32 devices in a mesh: az: 16 (over z, y, x), rad: 2 (over core).
Axes of the slice: x: 2, y: 2, z: 4, core: 2. Of those that a mesh axis runs over, the one named last changes fastest.
Arguments:
- state: float32 [5, 2, 512, 256], P(None, None, 'az', 'rad'), as said below
- shifts: int32 [256], P('rad'), may hold values from 4 to 96, as said below
Outputs:
- state_out: float32 [5, 2, 512, 256], P(None, None, 'az', 'rad')
The draws below stay inside these ranges and needn't reach their ends.
Inputs may be any that keep to these rules, and one draw needn't show every extreme that they name: `state`: density lies between 0.3 and 3, each velocity component (momentum over density) between -1 and 1, and energy exceeds the kinetic energy by at least 0.8 times density. `shifts`: both 4 and 96 occur.
All inputs are finite; a program needn't handle non-finite values.
Results may differ from the reference program's by a relative error of at most 0.0003.
Values sent between devices are 32-bit elements; how exact they have to be, the bound alone decides.
A program may use at most 64 MiB of HBM per device.

```python
import jax
import jax.numpy as jnp
from jax import lax

ZL = 2
STEPS = 2
SMIN = 4
SMAX = 96
NPHI = 512
NR = 256


def draw_state(key, part):
    shape = (ZL, NPHI, NR)
    key_density = jax.random.fold_in(key, 1)
    key_speed = jax.random.fold_in(key, 2)
    key_heat = jax.random.fold_in(key, 3)
    density = jnp.exp(jax.random.uniform(key_density, shape, jnp.float32, jnp.log(0.5), jnp.log(2.0)))
    speeds = jax.random.uniform(key_speed, (3,) + shape, jnp.float32, -1.0, 1.0)
    heat = jax.random.uniform(key_heat, shape, jnp.float32, 1.0, 2.0)
    momenta = density[None] * speeds
    energy = density * (heat + 0.5 * jnp.sum(speeds * speeds, axis=0))
    return jnp.concatenate([density[None], momenta, energy[None]], axis=0)


def draw_shifts(key, part):
    base = jax.random.randint(jax.random.fold_in(key, 11), (NR,), SMIN, SMAX + 1, dtype=jnp.int32)
    places = jax.random.permutation(jax.random.fold_in(key, 12), NR)[:6]
    planted = jnp.array([SMIN, 23, 42, 61, 80, SMAX], dtype=jnp.int32)
    return base.at[places].set(planted)


def setup_inputs(seed: int = 0) -> dict:
    key_of = jax.random.split(jax.random.key(seed), 3)
    state = draw_state(jax.random.fold_in(key_of[2], 71), 0)
    shifts = draw_shifts(jax.random.fold_in(key_of[2], 71), 0)
    return {"state": state, "shifts": shifts}


GAMMA_GAS = 1.4
COURANT_RADIAL = 0.15
COURANT_AZIMUTH = 0.15
VISCOSITY_COEF = 1.0


def cut(array, start, stop, axis):
    return lax.slice_in_dim(array, start, stop, axis=axis)


def van_leer(left_diff, right_diff):
    product = left_diff * right_diff
    positive = product > 0
    safe_sum = jnp.where(positive, left_diff + right_diff, 1.0)
    return jnp.where(positive, 2.0 * product / safe_sum, 0.0)


def transport(strip, axis, component, courant):
    length = strip.shape[axis] - 4
    velocity = strip[component:component + 1] / strip[0:1]
    diffs = cut(strip, 1, length + 4, axis) - cut(strip, 0, length + 3, axis)
    slopes = van_leer(cut(diffs, 0, length + 2, axis), cut(diffs, 1, length + 3, axis))
    left_state = cut(strip, 1, length + 2, axis) + 0.5 * cut(slopes, 0, length + 1, axis)
    right_state = cut(strip, 2, length + 3, axis) - 0.5 * cut(slopes, 1, length + 2, axis)
    face_speed = 0.5 * (cut(velocity, 1, length + 2, axis) + cut(velocity, 2, length + 3, axis))
    flux = jnp.maximum(face_speed, 0.0) * left_state + jnp.minimum(face_speed, 0.0) * right_state
    return -courant * (cut(flux, 1, length + 1, axis) - cut(flux, 0, length, axis))


def pressure_push(strip, axis, component, courant):
    length = strip.shape[axis] - 4
    density = strip[0:1]
    momenta = strip[1:4]
    speed = strip[component:component + 1] / density
    pressure = (GAMMA_GAS - 1.0) * (strip[4:5] - 0.5 * jnp.sum(momenta * momenta, axis=0, keepdims=True) / density)
    compress = jnp.minimum(cut(speed, 2, length + 4, axis) - cut(speed, 0, length + 2, axis), 0.0)
    total = cut(pressure, 1, length + 3, axis) + VISCOSITY_COEF * cut(density, 1, length + 3, axis) * compress * compress
    work = total * cut(speed, 1, length + 3, axis)
    gradient = 0.5 * (cut(total, 2, length + 2, axis) - cut(total, 0, length, axis))
    work_div = 0.5 * (cut(work, 2, length + 2, axis) - cut(work, 0, length, axis))
    zeros = jnp.zeros_like(gradient)
    pieces = [zeros, zeros, zeros, zeros, -courant * work_div]
    pieces[component] = -courant * gradient
    return jnp.concatenate(pieces, axis=0)


def hydro(state, az_strip, rad_strip):
    return state + transport(az_strip, 2, 2, COURANT_AZIMUTH) + transport(rad_strip, 3, 1, COURANT_RADIAL)


def viscous(state, az_strip, rad_strip):
    return state + pressure_push(az_strip, 2, 2, COURANT_AZIMUTH) + pressure_push(rad_strip, 3, 1, COURANT_RADIAL)


def strips(state):
    az_strip = jnp.pad(state, ((0, 0), (0, 0), (2, 2), (0, 0)), mode="wrap")
    rad_strip = jnp.pad(state, ((0, 0), (0, 0), (0, 0), (2, 2)), mode="edge")
    return az_strip, rad_strip


def rotate(state, shifts):
    total = state.shape[2]
    index = (jnp.arange(total, dtype=jnp.int32)[:, None] - shifts[None, :].astype(jnp.int32)) % total
    index = jnp.broadcast_to(index.astype(jnp.int32), state.shape)
    return jnp.take_along_axis(state, index, axis=2)


def reference(state, shifts):
    for step in range(STEPS):
        az_strip, rad_strip = strips(state)
        state = hydro(state, az_strip, rad_strip)
        state = rotate(state, shifts)
        az_strip, rad_strip = strips(state)
        state = viscous(state, az_strip, rad_strip)
    return state
```

```python
import functools

import jax
import jax.numpy as jnp
from jax import lax
from jax.experimental import pallas as pl
from jax.experimental.pallas import tpu as pltpu
from jax.sharding import PartitionSpec as P

STEPS = 2
SMAX = 96
EDGE = 4
TILE = 8

GAMMA_GAS = 1.4
COURANT_RADIAL = 0.15
COURANT_AZIMUTH = 0.15
VISCOSITY_COEF = 1.0


def up(x, axis):
    return pltpu.roll(x, x.shape[axis] - 1, axis)


def down(x, axis):
    return pltpu.roll(x, 1, axis)


def face_speeds(velocity, axis, courant):
    face = (0.5 * courant) * (velocity + up(velocity, axis))
    return jnp.maximum(face, 0.0), jnp.minimum(face, 0.0)


def advect(field, speeds, axis):
    low = field - down(field, axis)
    high = up(low, axis)
    product = low * high
    positive = product > 0
    half = jnp.where(positive, product / jnp.where(positive, low + high, 1.0), 0.0)
    flux = speeds[0] * (field + half) + speeds[1] * up(field - half, axis)
    return flux - down(flux, axis)


def push(pressure, density, speed, axis, courant):
    compress = jnp.minimum(up(speed, axis) - down(speed, axis), 0.0)
    total = pressure + VISCOSITY_COEF * density * compress * compress
    work = total * speed
    scale = -0.5 * courant
    return scale * (up(total, axis) - down(total, axis)), scale * (up(work, axis) - down(work, axis))


def shifted(window, shift_left, rows, longest):
    bits = longest.bit_length()
    x = window
    for bit in reversed(range(bits)):
        stride = 1 << bit
        left = stride - 1
        if stride >= TILE:
            keep = -(-(rows + left) // TILE) * TILE
            chosen = min(keep, x.shape[0] - stride)
            mask = (jnp.broadcast_to(shift_left, (chosen, shift_left.shape[1])) & stride) != 0
            y = jnp.where(mask, x[stride : stride + chosen], x[:chosen])
            x = y if chosen == keep else jnp.concatenate([y, x[chosen:keep]], axis=0)
        else:
            mask = (jnp.broadcast_to(shift_left, x.shape) & stride) != 0
            x = jnp.where(mask, pltpu.roll(x, x.shape[0] - stride, 0), x)
    return x[:rows]


def kernel(n_az, n_rad, x, shifts, out, *scratch):
    (A, W0, W1, O0, O1, L0, R0, L1, R1, L2, R2, state_send, state_recv, gather_send, gather_recv,
     side_send, side_recv) = scratch
    fields, depth, width, lanes = x.shape
    behind = SMAX + EDGE
    whole = behind // width
    tail = behind % width
    tail_rows = -(-tail // TILE) * TILE
    base = tail_rows + whole * width
    hops = whole + (1 if tail else 0)
    me = lax.axis_index("az")
    position = lax.axis_index("rad")

    def az(by):
        return {"az": lax.rem(me + by + n_az, n_az)}

    def rad(by):
        return {"rad": position + by}

    barrier = pltpu.get_barrier_semaphore()
    MESH = pl.DeviceIdType.MESH
    for h in range(1, hops + 1):
        pl.semaphore_signal(barrier, inc=1, device_id=az(-h), device_id_type=MESH)
    pl.semaphore_signal(barrier, inc=1, device_id=az(1), device_id_type=MESH)

    has_left = position > 0
    has_right = position < n_rad - 1

    @pl.when(has_left)
    def _():
        pl.semaphore_signal(barrier, inc=1, device_id=rad(-1), device_id_type=MESH)

    @pl.when(has_right)
    def _():
        pl.semaphore_signal(barrier, inc=1, device_id=rad(1), device_id_type=MESH)

    A[:, :, TILE : TILE + width, :] = x[...]
    beside_me = (position + n_rad - 1) // n_rad + (2 * n_rad - 2 - position) // n_rad
    pl.semaphore_wait(barrier, hops + 1 + beside_me)

    def remote(src, dst, send, recv, where):
        return pltpu.make_async_remote_copy(
            src_ref=src, dst_ref=dst, send_sem=send, recv_sem=recv, device_id=where, device_id_type=MESH
        )

    def ring_copies(z):
        return [
            remote(x.at[:, z, width - TILE : width], A.at[:, z, 0:TILE],
                   state_send.at[0, z], state_recv.at[0, z], az(1)),
            remote(x.at[:, z, 0:TILE], A.at[:, z, TILE + width : 2 * TILE + width],
                   state_send.at[1, z], state_recv.at[1, z], az(-1)),
        ]

    def side_copies(phase, src, left_dst, right_dst, z):
        to_right = remote(src.at[:, z], left_dst.at[:, z], side_send.at[phase, 0, z],
                          side_recv.at[phase, 0, z], rad(1))
        to_left = remote(src.at[:, z], right_dst.at[:, z], side_send.at[phase, 1, z],
                         side_recv.at[phase, 1, z], rad(-1))
        return to_right, to_left

    def start_side(*args):
        to_right, to_left = side_copies(*args)

        @pl.when(has_right)
        def _():
            to_right.start()

        @pl.when(has_left)
        def _():
            to_left.start()

    def await_side(*args):
        to_right, to_left = side_copies(*args)

        @pl.when(has_left)
        def _():
            to_right.wait_recv()

        @pl.when(has_right)
        def _():
            to_left.wait_recv()

    def end_side(*args):
        to_right, to_left = side_copies(*args)

        @pl.when(has_right)
        def _():
            to_right.wait_send()

        @pl.when(has_left)
        def _():
            to_left.wait_send()

    windows = (W0, W1)
    rotated = (O0, O1)
    sides = ((x, L0, R0), (O0, L1, R1), (O1, L2, R2))

    def gather_copies(step, z):
        W = windows[step]
        copies = []
        for h in range(hops, 0, -1):
            if h > whole:
                src = W.at[:, z, base + width - tail_rows : base + width]
                dst = W.at[:, z, 0:tail_rows]
            else:
                src = W.at[:, z, base : base + width]
                dst = W.at[:, z, base - h * width : base - (h - 1) * width]
            copies.append(remote(src, dst, gather_send.at[step, h - 1, z], gather_recv.at[step, h - 1, z], az(h)))
        return copies

    def edges(own, left, right):
        rows = own.shape[0]
        lane = lax.broadcasted_iota(jnp.int32, (rows, lanes), 1)
        at = jnp.full((rows, lanes), position, jnp.int32)
        left = jnp.where(at == 0, jnp.broadcast_to(own[:, 0:1], own.shape), left)
        right = jnp.where(at == n_rad - 1, jnp.broadcast_to(own[:, lanes - 1 : lanes], own.shape), right)
        return jnp.where(lane < lanes // 2, right, left)

    def wide(own, beside):
        return jnp.concatenate([own, beside], axis=1)

    def hydro(step, z, strip, beside):
        rows = slice(TILE, TILE + width)
        tall = [strip(f) for f in range(fields)]
        az_speeds = face_speeds(tall[2] / tall[0], 0, COURANT_AZIMUTH)
        broad = [wide(tall[f][rows], beside(f, tall[f][rows])) for f in range(fields)]
        rad_speeds = face_speeds(broad[1] / broad[0], 1, COURANT_RADIAL)
        for f in range(fields):
            along = advect(tall[f], az_speeds, 0)[rows]
            across = advect(broad[f], rad_speeds, 1)[:, :lanes]
            windows[step][f, z, base : base + width, :] = tall[f][rows] - along - across
        for copy in gather_copies(step, z):
            copy.start()

    def viscous(z, state, extended):
        rho, mr, mp, mz, energy = state
        own = slice(None) if extended else slice(0, lanes)
        inverse = 1.0 / rho
        pressure = (GAMMA_GAS - 1.0) * (energy - 0.5 * (mr * mr + mp * mp + mz * mz) * inverse)
        az_m, az_e = push(pressure[:, own], rho[:, own], (mp * inverse)[:, own], 0, COURANT_AZIMUTH)
        rad_m, rad_e = push(pressure, rho, mr * inverse, 1, COURANT_RADIAL)
        return [
            rho[:, own],
            mr[:, own] + rad_m[:, own],
            mp[:, own] + az_m,
            mz[:, own],
            energy[:, own] + az_e + rad_e[:, own],
        ]

    count = width + 2 * EDGE

    for z in range(depth):
        for copy in ring_copies(z):
            copy.start()
        start_side(0, *sides[0], z)

    for z in range(depth):
        for copy in ring_copies(z):
            copy.wait_recv()
        await_side(0, *sides[0], z)
        hydro(0, z, lambda f: A[f, z], lambda f, own: edges(own, L0[f, z], R0[f, z]))

    for step in range(STEPS):
        O, L, R = sides[step + 1]
        for z in range(depth):
            for copy in gather_copies(step, z):
                copy.wait_recv()
            for f in range(fields):
                O[f, z] = shifted(windows[step][f, z], base - EDGE - shifts[...], count, base - EDGE - 4)
            start_side(step + 1, O, L, R, z)
        for z in range(depth):
            await_side(step + 1, O, L, R, z)
            state = [wide(O[f, z], edges(O[f, z], L[f, z], R[f, z])) for f in range(fields)]
            if step == STEPS - 1:
                new = viscous(z, state, False)
                for f in range(fields):
                    out[f, z] = new[f][EDGE : EDGE + width]
            else:
                new = viscous(z, state, True)
                A_rows = slice(TILE - EDGE, TILE - EDGE + count)
                for f in range(fields):
                    A[f, z, A_rows, :] = new[f][:, :lanes]
                hydro(
                    step + 1,
                    z,
                    lambda f: A[f, z],
                    lambda f, own: edges(own, *[new[f][EDGE : EDGE + width, lanes:]] * 2),
                )

    for z in range(depth):
        for copy in ring_copies(z):
            copy.wait_send()
        for phase in range(STEPS + 1):
            end_side(phase, *sides[phase], z)
        for step in range(STEPS):
            for copy in gather_copies(step, z):
                copy.wait_send()


def body(mesh, state, shifts):
    n_az, n_rad = mesh.shape["az"], mesh.shape["rad"]
    fields, depth, width, lanes = state.shape
    behind = SMAX + EDGE
    base = -(-(behind % width) // TILE) * TILE + behind // width * width
    hops = -(-behind // width)
    count = width + 2 * EDGE
    vmem = lambda rows: pltpu.VMEM((fields, depth, rows, lanes), jnp.float32)
    dma = pltpu.SemaphoreType.DMA
    return pl.pallas_call(
        functools.partial(kernel, n_az, n_rad),
        out_shape=jax.ShapeDtypeStruct(state.shape, state.dtype),
        in_specs=[pl.BlockSpec(memory_space=pltpu.VMEM)] * 2,
        out_specs=pl.BlockSpec(memory_space=pltpu.VMEM),
        scratch_shapes=[
            vmem(width + 2 * TILE),
            vmem(base + width),
            vmem(base + width),
            vmem(count),
            vmem(count),
            vmem(width),
            vmem(width),
            vmem(count),
            vmem(count),
            vmem(count),
            vmem(count),
            dma((2, depth)),
            dma((2, depth)),
            dma((STEPS, hops, depth)),
            dma((STEPS, hops, depth)),
            dma((STEPS + 1, 2, depth)),
            dma((STEPS + 1, 2, depth)),
        ],
        compiler_params=pltpu.CompilerParams(collective_id=0, has_side_effects=True),
    )(state, shifts.reshape(1, -1))


def solution(mesh):
    in_specs = (P(None, None, "az", "rad"), P("rad"))
    out_specs = P(None, None, "az", "rad")
    return jax.shard_map(
        functools.partial(body, mesh), mesh=mesh, in_specs=in_specs, out_specs=out_specs, check_vma=False
    )
```

```python
import functools

import jax
import jax.numpy as jnp
from jax import lax
from jax.experimental import pallas as pl
from jax.experimental.pallas import tpu as pltpu
from jax.sharding import PartitionSpec as P

STEPS = 2
SMIN = 4
SMAX = 96
EDGE = 4
TILE = 8

GAMMA_GAS = 1.4
COURANT_RADIAL = 0.15
COURANT_AZIMUTH = 0.15
VISCOSITY_COEF = 1.0


def up(x, axis):
    return pltpu.roll(x, x.shape[axis] - 1, axis)


def down(x, axis):
    return pltpu.roll(x, 1, axis)


def face_speeds(velocity, axis, courant):
    face = (0.5 * courant) * (velocity + up(velocity, axis))
    return jnp.maximum(face, 0.0), jnp.minimum(face, 0.0)


def advect(field, speeds, axis):
    low = field - down(field, axis)
    high = up(low, axis)
    product = low * high
    positive = product > 0
    half = jnp.where(positive, product / jnp.where(positive, low + high, 1.0), 0.0)
    flux = speeds[0] * (field + half) + speeds[1] * up(field - half, axis)
    return flux - down(flux, axis)


def push(pressure, density, speed, axis, courant):
    compress = jnp.minimum(up(speed, axis) - down(speed, axis), 0.0)
    total = pressure + VISCOSITY_COEF * density * compress * compress
    work = total * speed
    scale = -0.5 * courant
    return scale * (up(total, axis) - down(total, axis)), scale * (up(work, axis) - down(work, axis))


def shifted(window, shift_left, rows, longest):
    bits = longest.bit_length()
    x = window
    for bit in reversed(range(bits)):
        stride = 1 << bit
        left = stride - 1
        if stride >= TILE:
            keep = -(-(rows + left) // TILE) * TILE
            chosen = min(keep, x.shape[0] - stride)
            mask = (jnp.broadcast_to(shift_left, (chosen, shift_left.shape[1])) & stride) != 0
            y = jnp.where(mask, x[stride : stride + chosen], x[:chosen])
            x = y if chosen == keep else jnp.concatenate([y, x[chosen:keep]], axis=0)
        else:
            mask = (jnp.broadcast_to(shift_left, x.shape) & stride) != 0
            x = jnp.where(mask, pltpu.roll(x, x.shape[0] - stride, 0), x)
    return x[:rows]


def kernel(n_az, n_rad, x, shifts, out, *scratch):
    (A, W0, W1, O0, O1, L0, R0, L1, R1, L2, R2, state_send, state_recv, gather_send, gather_recv,
     side_send, side_recv) = scratch
    fields, depth, width, lanes = x.shape
    behind = SMAX + EDGE
    whole = behind // width
    tail = behind % width
    tail_rows = -(-tail // TILE) * TILE
    group = whole + 1
    base = group * width
    first_row = width - tail_rows
    me = lax.axis_index("az")
    place = lax.rem(me, group)
    position = lax.axis_index("rad")

    def az(by):
        return {"az": lax.rem(me + by + n_az, n_az)}

    def member(by):
        return {"az": me - place + lax.rem(place + by, group)}

    def rad(by):
        return {"rad": position + by}

    barrier = pltpu.get_barrier_semaphore()
    MESH = pl.DeviceIdType.MESH
    for by in (1, -1, -group):
        pl.semaphore_signal(barrier, inc=1, device_id=az(by), device_id_type=MESH)
    for h in range(1, group):
        pl.semaphore_signal(barrier, inc=1, device_id=member(h), device_id_type=MESH)

    has_left = position > 0
    has_right = position < n_rad - 1

    @pl.when(has_left)
    def _():
        pl.semaphore_signal(barrier, inc=1, device_id=rad(-1), device_id_type=MESH)

    @pl.when(has_right)
    def _():
        pl.semaphore_signal(barrier, inc=1, device_id=rad(1), device_id_type=MESH)

    A[:, :, TILE : TILE + width, :] = x[...]
    beside_me = (position + n_rad - 1) // n_rad + (2 * n_rad - 2 - position) // n_rad
    pl.semaphore_wait(barrier, group + 2 + beside_me)

    def remote(src, dst, send, recv, where):
        return pltpu.make_async_remote_copy(
            src_ref=src, dst_ref=dst, send_sem=send, recv_sem=recv, device_id=where, device_id_type=MESH
        )

    def ring_copies(z):
        return [
            remote(x.at[:, z, width - TILE : width], A.at[:, z, 0:TILE],
                   state_send.at[0, z], state_recv.at[0, z], az(1)),
            remote(x.at[:, z, 0:TILE], A.at[:, z, TILE + width : 2 * TILE + width],
                   state_send.at[1, z], state_recv.at[1, z], az(-1)),
        ]

    def side_copies(phase, src, left_dst, right_dst, z):
        to_right = remote(src.at[:, z], left_dst.at[:, z], side_send.at[phase, 0, z],
                          side_recv.at[phase, 0, z], rad(1))
        to_left = remote(src.at[:, z], right_dst.at[:, z], side_send.at[phase, 1, z],
                         side_recv.at[phase, 1, z], rad(-1))
        return to_right, to_left

    def start_side(*args):
        to_right, to_left = side_copies(*args)

        @pl.when(has_right)
        def _():
            to_right.start()

        @pl.when(has_left)
        def _():
            to_left.start()

    def await_side(*args):
        to_right, to_left = side_copies(*args)

        @pl.when(has_left)
        def _():
            to_right.wait_recv()

        @pl.when(has_right)
        def _():
            to_left.wait_recv()

    def end_side(*args):
        to_right, to_left = side_copies(*args)

        @pl.when(has_right)
        def _():
            to_right.wait_send()

        @pl.when(has_left)
        def _():
            to_left.wait_send()

    windows = (W0, W1)
    rotated = (O0, O1)
    sides = ((x, L0, R0), (O0, L1, R1), (O1, L2, R2))

    def gather_copies(step, f, z):
        W = windows[step]
        own, back = W.at[f, z, base : base + width], W.at[f, z, 0:width]
        sems = lambda h: (gather_send.at[step, h, f, z], gather_recv.at[step, h, f, z])
        onward = remote(own, back, *sems(0), az(group))
        inside = []
        for h in range(1, group):
            dst = W.at[f, z, base - h * width : base - (h - 1) * width]
            inside.append([remote(src, dst, *sems(h), member(h)) for src in (own, back)])
        return onward, inside

    def send_own(step, f, z):
        onward, inside = gather_copies(step, f, z)
        onward.start()
        for h in range(1, group):

            @pl.when(place + h < group)
            def _():
                inside[h - 1][0].start()

    def pass_on(step, f, z):
        onward, inside = gather_copies(step, f, z)
        onward.wait_recv()
        for h in range(1, group):

            @pl.when(place + h >= group)
            def _():
                inside[h - 1][1].start()

    def edges(own, left, right):
        rows = own.shape[0]
        lane = lax.broadcasted_iota(jnp.int32, (rows, lanes), 1)
        at = jnp.full((rows, lanes), position, jnp.int32)
        left = jnp.where(at == 0, jnp.broadcast_to(own[:, 0:1], own.shape), left)
        right = jnp.where(at == n_rad - 1, jnp.broadcast_to(own[:, lanes - 1 : lanes], own.shape), right)
        return jnp.where(lane < lanes // 2, right, left)

    def wide(own, beside):
        return jnp.concatenate([own, beside], axis=1)

    def hydro(step, z, strip, beside):
        rows = slice(TILE, TILE + width)
        tall = [strip(f) for f in range(fields)]
        az_speeds = face_speeds(tall[2] / tall[0], 0, COURANT_AZIMUTH)
        broad = [wide(tall[f][rows], beside(f, tall[f][rows])) for f in range(fields)]
        rad_speeds = face_speeds(broad[1] / broad[0], 1, COURANT_RADIAL)
        for f in range(fields):
            along = advect(tall[f], az_speeds, 0)[rows]
            across = advect(broad[f], rad_speeds, 1)[:, :lanes]
            windows[step][f, z, base : base + width, :] = tall[f][rows] - along - across
            send_own(step, f, z)

    def viscous(z, state, extended):
        rho, mr, mp, mz, energy = state
        own = slice(None) if extended else slice(0, lanes)
        inverse = 1.0 / rho
        pressure = (GAMMA_GAS - 1.0) * (energy - 0.5 * (mr * mr + mp * mp + mz * mz) * inverse)
        az_m, az_e = push(pressure[:, own], rho[:, own], (mp * inverse)[:, own], 0, COURANT_AZIMUTH)
        rad_m, rad_e = push(pressure, rho, mr * inverse, 1, COURANT_RADIAL)
        return [
            rho[:, own],
            mr[:, own] + rad_m[:, own],
            mp[:, own] + az_m,
            mz[:, own],
            energy[:, own] + az_e + rad_e[:, own],
        ]

    count = width + 2 * EDGE

    for z in range(depth):
        for copy in ring_copies(z):
            copy.start()
        start_side(0, *sides[0], z)

    for z in range(depth):
        for copy in ring_copies(z):
            copy.wait_recv()
        await_side(0, *sides[0], z)
        hydro(0, z, lambda f: A[f, z], lambda f, own: edges(own, L0[f, z], R0[f, z]))

    for step in range(STEPS):
        for z in range(depth):
            for f in range(fields):
                pass_on(step, f, z)
        O, L, R = sides[step + 1]
        for z in range(depth):
            for f in range(fields):
                for copies in gather_copies(step, f, z)[1]:
                    copies[0].wait_recv()
                start = base - first_row - EDGE
                O[f, z] = shifted(windows[step][f, z, first_row:], start - shifts[...], count, start - SMIN)
            start_side(step + 1, O, L, R, z)
        for z in range(depth):
            await_side(step + 1, O, L, R, z)
            state = [wide(O[f, z], edges(O[f, z], L[f, z], R[f, z])) for f in range(fields)]
            if step == STEPS - 1:
                new = viscous(z, state, False)
                for f in range(fields):
                    out[f, z] = new[f][EDGE : EDGE + width]
            else:
                new = viscous(z, state, True)
                A_rows = slice(TILE - EDGE, TILE - EDGE + count)
                for f in range(fields):
                    A[f, z, A_rows, :] = new[f][:, :lanes]
                hydro(
                    step + 1,
                    z,
                    lambda f: A[f, z],
                    lambda f, own: edges(own, *[new[f][EDGE : EDGE + width, lanes:]] * 2),
                )

    for z in range(depth):
        for copy in ring_copies(z):
            copy.wait_send()
        for phase in range(STEPS + 1):
            end_side(phase, *sides[phase], z)
        for step in range(STEPS):
            for f in range(fields):
                onward, inside = gather_copies(step, f, z)
                onward.wait_send()
                for copies in inside:
                    copies[0].wait_send()


def body(mesh, state, shifts):
    n_az, n_rad = mesh.shape["az"], mesh.shape["rad"]
    fields, depth, width, lanes = state.shape
    behind = SMAX + EDGE
    group = behind // width + 1
    window = (group + 1) * width
    count = width + 2 * EDGE
    vmem = lambda rows: pltpu.VMEM((fields, depth, rows, lanes), jnp.float32)
    dma = pltpu.SemaphoreType.DMA
    return pl.pallas_call(
        functools.partial(kernel, n_az, n_rad),
        out_shape=jax.ShapeDtypeStruct(state.shape, state.dtype),
        in_specs=[pl.BlockSpec(memory_space=pltpu.VMEM)] * 2,
        out_specs=pl.BlockSpec(memory_space=pltpu.VMEM),
        scratch_shapes=[
            vmem(width + 2 * TILE),
            vmem(window),
            vmem(window),
            vmem(count),
            vmem(count),
            vmem(width),
            vmem(width),
            vmem(count),
            vmem(count),
            vmem(count),
            vmem(count),
            dma((2, depth)),
            dma((2, depth)),
            dma((STEPS, group, fields, depth)),
            dma((STEPS, group, fields, depth)),
            dma((STEPS + 1, 2, depth)),
            dma((STEPS + 1, 2, depth)),
        ],
        compiler_params=pltpu.CompilerParams(collective_id=0, has_side_effects=True),
    )(state, shifts.reshape(1, -1))


def solution(mesh):
    in_specs = (P(None, None, "az", "rad"), P("rad"))
    out_specs = P(None, None, "az", "rad")
    return jax.shard_map(
        functools.partial(body, mesh), mesh=mesh, in_specs=in_specs, out_specs=out_specs, check_vma=False
    )
```

```python
import functools

import jax
import jax.numpy as jnp
from jax import lax
from jax.experimental import pallas as pl
from jax.experimental.pallas import tpu as pltpu
from jax.sharding import PartitionSpec as P

STEPS = 2
SMIN = 4
SMAX = 96
EDGE = 4
TILE = 8

GAMMA_GAS = 1.4
COURANT_RADIAL = 0.15
COURANT_AZIMUTH = 0.15
VISCOSITY_COEF = 1.0


def up(x, axis):
    return pltpu.roll(x, x.shape[axis] - 1, axis)


def down(x, axis):
    return pltpu.roll(x, 1, axis)


def face_speeds(velocity, axis, courant):
    face = (0.5 * courant) * (velocity + up(velocity, axis))
    return jnp.maximum(face, 0.0), jnp.minimum(face, 0.0)


def advect(field, speeds, axis):
    low = field - down(field, axis)
    high = up(low, axis)
    product = low * high
    positive = product > 0
    half = jnp.where(positive, product / jnp.where(positive, low + high, 1.0), 0.0)
    flux = speeds[0] * (field + half) + speeds[1] * up(field - half, axis)
    return flux - down(flux, axis)


def push(pressure, density, speed, axis, courant):
    compress = jnp.minimum(up(speed, axis) - down(speed, axis), 0.0)
    total = pressure + VISCOSITY_COEF * density * compress * compress
    work = total * speed
    scale = -0.5 * courant
    return scale * (up(total, axis) - down(total, axis)), scale * (up(work, axis) - down(work, axis))


def shifted(window, shift_left, rows, longest):
    bits = longest.bit_length()
    x = window
    for bit in reversed(range(bits)):
        stride = 1 << bit
        left = stride - 1
        if stride >= TILE:
            keep = -(-(rows + left) // TILE) * TILE
            chosen = min(keep, x.shape[0] - stride)
            mask = (jnp.broadcast_to(shift_left, (chosen, shift_left.shape[1])) & stride) != 0
            y = jnp.where(mask, x[stride : stride + chosen], x[:chosen])
            x = y if chosen == keep else jnp.concatenate([y, x[chosen:keep]], axis=0)
        else:
            mask = (jnp.broadcast_to(shift_left, x.shape) & stride) != 0
            x = jnp.where(mask, pltpu.roll(x, x.shape[0] - stride, 0), x)
    return x[:rows]


def kernel(n_az, n_rad, x_in, shifts, out, *scratch):
    (x, LOW, HIGH, load_sem, A, W0, W1, O0, O1, L0, R0, L1, R1, L2, R2, state_send, state_recv, relay_send, relay_recv, gather_send, gather_recv,
     side_send, side_recv) = scratch
    fields, depth, width, lanes = x.shape
    behind = SMAX + EDGE
    whole = behind // width
    tail = behind % width
    tail_rows = -(-tail // TILE) * TILE
    group = whole + 1
    base = group * width
    first_row = width - tail_rows
    me = lax.axis_index("az")
    place = lax.rem(me, group)
    position = lax.axis_index("rad")

    def az(by):
        return {"az": lax.rem(me + by + n_az, n_az)}

    def member(by):
        return {"az": me - place + lax.rem(place + by + group, group)}

    def rad(by):
        return {"rad": position + by}

    barrier = pltpu.get_barrier_semaphore()
    MESH = pl.DeviceIdType.MESH
    load = pltpu.make_async_copy(x_in, x, load_sem)
    load.start()
    for by in (group, -group):
        pl.semaphore_signal(barrier, inc=1, device_id=az(by), device_id_type=MESH)
    for h in range(1, group):
        pl.semaphore_signal(barrier, inc=1, device_id=member(h), device_id_type=MESH)

    has_left = position > 0
    has_right = position < n_rad - 1

    @pl.when(has_left)
    def _():
        pl.semaphore_signal(barrier, inc=1, device_id=rad(-1), device_id_type=MESH)

    @pl.when(has_right)
    def _():
        pl.semaphore_signal(barrier, inc=1, device_id=rad(1), device_id_type=MESH)

    load.wait()
    A[:, :, TILE : TILE + width, :] = x[...]
    beside_me = (position + n_rad - 1) // n_rad + (2 * n_rad - 2 - position) // n_rad
    pl.semaphore_wait(barrier, group + 1 + beside_me)

    def remote(src, dst, send, recv, where):
        return pltpu.make_async_remote_copy(
            src_ref=src, dst_ref=dst, send_sem=send, recv_sem=recv, device_id=where, device_id_type=MESH
        )

    def ring_copies(z):
        pairs = []
        for side, relayed, by, rows, dst in (
            (0, LOW, 1, slice(width - TILE, width), slice(0, TILE)),
            (1, HIGH, -1, slice(0, TILE), slice(TILE + width, 2 * TILE + width)),
        ):
            own = x.at[:, z, rows]
            onward = remote(own, relayed.at[:, z], relay_send.at[side, z], relay_recv.at[side, z], az(by * group))
            sems = state_send.at[side, z], state_recv.at[side, z]
            inside = [remote(src, A.at[:, z, dst], *sems, member(by)) for src in (own, relayed.at[:, z])]
            pairs.append((place == (group - 1 if by == 1 else 0), onward, inside))
        return pairs

    def start_ring(z):
        for last, onward, inside in ring_copies(z):

            @pl.when(last)
            def _():
                onward.start()

            @pl.when(jnp.logical_not(last))
            def _():
                inside[0].start()

    def relay_ring(z):
        for last, onward, inside in ring_copies(z):

            @pl.when(last)
            def _():
                onward.wait_recv()
                inside[1].start()

    def end_ring(z):
        for last, onward, inside in ring_copies(z):
            inside[0].wait_send()

            @pl.when(last)
            def _():
                onward.wait_send()

    def side_copies(phase, src, left_dst, right_dst, z):
        to_right = remote(src.at[:, z], left_dst.at[:, z], side_send.at[phase, 0, z],
                          side_recv.at[phase, 0, z], rad(1))
        to_left = remote(src.at[:, z], right_dst.at[:, z], side_send.at[phase, 1, z],
                         side_recv.at[phase, 1, z], rad(-1))
        return to_right, to_left

    def start_side(*args):
        to_right, to_left = side_copies(*args)

        @pl.when(has_right)
        def _():
            to_right.start()

        @pl.when(has_left)
        def _():
            to_left.start()

    def await_side(*args):
        to_right, to_left = side_copies(*args)

        @pl.when(has_left)
        def _():
            to_right.wait_recv()

        @pl.when(has_right)
        def _():
            to_left.wait_recv()

    def end_side(*args):
        to_right, to_left = side_copies(*args)

        @pl.when(has_right)
        def _():
            to_right.wait_send()

        @pl.when(has_left)
        def _():
            to_left.wait_send()

    windows = (W0, W1)
    rotated = (O0, O1)
    sides = ((x, L0, R0), (O0, L1, R1), (O1, L2, R2))

    def gather_copies(step, f, z):
        W = windows[step]
        own, back = W.at[f, z, base : base + width], W.at[f, z, 0:width]
        sems = lambda h: (gather_send.at[step, h, f, z], gather_recv.at[step, h, f, z])
        onward = remote(own, back, *sems(0), az(group))
        inside = []
        for h in range(1, group):
            dst = W.at[f, z, base - h * width : base - (h - 1) * width]
            inside.append([remote(src, dst, *sems(h), member(h)) for src in (own, back)])
        return onward, inside

    def send_own(step, f, z):
        onward, inside = gather_copies(step, f, z)
        onward.start()
        for h in range(1, group):

            @pl.when(place + h < group)
            def _():
                inside[h - 1][0].start()

    def pass_on(step, f, z):
        onward, inside = gather_copies(step, f, z)
        onward.wait_recv()
        for h in range(1, group):

            @pl.when(place + h >= group)
            def _():
                inside[h - 1][1].start()

    def edges(own, left, right):
        rows = own.shape[0]
        lane = lax.broadcasted_iota(jnp.int32, (rows, lanes), 1)
        at = jnp.full((rows, lanes), position, jnp.int32)
        left = jnp.where(at == 0, jnp.broadcast_to(own[:, 0:1], own.shape), left)
        right = jnp.where(at == n_rad - 1, jnp.broadcast_to(own[:, lanes - 1 : lanes], own.shape), right)
        return jnp.where(lane < lanes // 2, right, left)

    def wide(own, beside):
        return jnp.concatenate([own, beside], axis=1)

    def hydro(step, z, strip, beside):
        rows = slice(TILE, TILE + width)
        tall = [strip(f) for f in range(fields)]
        az_speeds = face_speeds(tall[2] / tall[0], 0, COURANT_AZIMUTH)
        broad = [wide(tall[f][rows], beside(f, tall[f][rows])) for f in range(fields)]
        rad_speeds = face_speeds(broad[1] / broad[0], 1, COURANT_RADIAL)
        for f in range(fields):
            along = advect(tall[f], az_speeds, 0)[rows]
            across = advect(broad[f], rad_speeds, 1)[:, :lanes]
            windows[step][f, z, base : base + width, :] = tall[f][rows] - along - across
            send_own(step, f, z)

    def viscous(z, state, extended):
        rho, mr, mp, mz, energy = state
        own = slice(None) if extended else slice(0, lanes)
        inverse = 1.0 / rho
        pressure = (GAMMA_GAS - 1.0) * (energy - 0.5 * (mr * mr + mp * mp + mz * mz) * inverse)
        az_m, az_e = push(pressure[:, own], rho[:, own], (mp * inverse)[:, own], 0, COURANT_AZIMUTH)
        rad_m, rad_e = push(pressure, rho, mr * inverse, 1, COURANT_RADIAL)
        return [
            rho[:, own],
            mr[:, own] + rad_m[:, own],
            mp[:, own] + az_m,
            mz[:, own],
            energy[:, own] + az_e + rad_e[:, own],
        ]

    count = width + 2 * EDGE

    for z in range(depth):
        start_ring(z)
    for z in range(depth):
        start_side(0, *sides[0], z)
    for z in range(depth):
        relay_ring(z)

    for z in range(depth):
        for _, _, inside in ring_copies(z):
            inside[0].wait_recv()
        await_side(0, *sides[0], z)
        hydro(0, z, lambda f: A[f, z], lambda f, own: edges(own, L0[f, z], R0[f, z]))

    for step in range(STEPS):
        for z in range(depth):
            for f in range(fields):
                pass_on(step, f, z)
        O, L, R = sides[step + 1]
        for z in range(depth):
            for f in range(fields):
                for copies in gather_copies(step, f, z)[1]:
                    copies[0].wait_recv()
                start = base - first_row - EDGE
                O[f, z] = shifted(windows[step][f, z, first_row:], start - shifts[...], count, start - SMIN)
            start_side(step + 1, O, L, R, z)
        for z in range(depth):
            await_side(step + 1, O, L, R, z)
            state = [wide(O[f, z], edges(O[f, z], L[f, z], R[f, z])) for f in range(fields)]
            if step == STEPS - 1:
                new = viscous(z, state, False)
                for f in range(fields):
                    out[f, z] = new[f][EDGE : EDGE + width]
            else:
                new = viscous(z, state, True)
                A_rows = slice(TILE - EDGE, TILE - EDGE + count)
                for f in range(fields):
                    A[f, z, A_rows, :] = new[f][:, :lanes]
                hydro(
                    step + 1,
                    z,
                    lambda f: A[f, z],
                    lambda f, own: edges(own, *[new[f][EDGE : EDGE + width, lanes:]] * 2),
                )

    for z in range(depth):
        end_ring(z)
        for phase in range(STEPS + 1):
            end_side(phase, *sides[phase], z)
        for step in range(STEPS):
            for f in range(fields):
                onward, inside = gather_copies(step, f, z)
                onward.wait_send()
                for copies in inside:
                    copies[0].wait_send()


def body(mesh, state, shifts):
    n_az, n_rad = mesh.shape["az"], mesh.shape["rad"]
    fields, depth, width, lanes = state.shape
    behind = SMAX + EDGE
    group = behind // width + 1
    window = (group + 1) * width
    count = width + 2 * EDGE
    vmem = lambda rows: pltpu.VMEM((fields, depth, rows, lanes), jnp.float32)
    dma = pltpu.SemaphoreType.DMA
    return pl.pallas_call(
        functools.partial(kernel, n_az, n_rad),
        out_shape=jax.ShapeDtypeStruct(state.shape, state.dtype),
        in_specs=[pl.BlockSpec(memory_space=pl.ANY), pl.BlockSpec(memory_space=pltpu.VMEM)],
        out_specs=pl.BlockSpec(memory_space=pltpu.VMEM),
        scratch_shapes=[
            vmem(width),
            vmem(TILE),
            vmem(TILE),
            dma(()),
            vmem(width + 2 * TILE),
            vmem(window),
            vmem(window),
            vmem(count),
            vmem(count),
            vmem(width),
            vmem(width),
            vmem(count),
            vmem(count),
            vmem(count),
            vmem(count),
            dma((2, depth)),
            dma((2, depth)),
            dma((2, depth)),
            dma((2, depth)),
            dma((STEPS, group, fields, depth)),
            dma((STEPS, group, fields, depth)),
            dma((STEPS + 1, 2, depth)),
            dma((STEPS + 1, 2, depth)),
        ],
        compiler_params=pltpu.CompilerParams(collective_id=0, has_side_effects=True),
    )(state, shifts.reshape(1, -1))


def solution(mesh):
    in_specs = (P(None, None, "az", "rad"), P("rad"))
    out_specs = P(None, None, "az", "rad")
    return jax.shard_map(
        functools.partial(body, mesh), mesh=mesh, in_specs=in_specs, out_specs=out_specs, check_vma=False
    )
```

```python
import functools

import jax
import jax.numpy as jnp
from jax import lax
from jax.experimental import pallas as pl
from jax.experimental.pallas import tpu as pltpu
from jax.sharding import PartitionSpec as P

STEPS = 2
SMIN = 4
SMAX = 96
EDGE = 4
TILE = 8

GAMMA_GAS = 1.4
COURANT_RADIAL = 0.15
COURANT_AZIMUTH = 0.15
VISCOSITY_COEF = 1.0


def up(x, axis):
    return pltpu.roll(x, x.shape[axis] - 1, axis)


def down(x, axis):
    return pltpu.roll(x, 1, axis)


def face_speeds(velocity, axis, courant):
    face = (0.5 * courant) * (velocity + up(velocity, axis))
    return jnp.maximum(face, 0.0), jnp.minimum(face, 0.0)


def advect(field, speeds, axis):
    low = field - down(field, axis)
    high = up(low, axis)
    product = low * high
    positive = product > 0
    half = jnp.where(positive, product / jnp.where(positive, low + high, 1.0), 0.0)
    flux = speeds[0] * (field + half) + speeds[1] * up(field - half, axis)
    return flux - down(flux, axis)


def push(pressure, density, speed, axis, courant):
    compress = jnp.minimum(up(speed, axis) - down(speed, axis), 0.0)
    total = pressure + VISCOSITY_COEF * density * compress * compress
    work = total * speed
    scale = -0.5 * courant
    return scale * (up(total, axis) - down(total, axis)), scale * (up(work, axis) - down(work, axis))


def shifted(window, shift_left, rows, longest):
    bits = longest.bit_length()
    x = window
    for bit in reversed(range(bits)):
        stride = 1 << bit
        left = stride - 1
        if stride >= TILE:
            keep = -(-(rows + left) // TILE) * TILE
            chosen = min(keep, x.shape[0] - stride)
            mask = (jnp.broadcast_to(shift_left, (chosen, shift_left.shape[1])) & stride) != 0
            y = jnp.where(mask, x[stride : stride + chosen], x[:chosen])
            x = y if chosen == keep else jnp.concatenate([y, x[chosen:keep]], axis=0)
        else:
            mask = (jnp.broadcast_to(shift_left, x.shape) & stride) != 0
            x = jnp.where(mask, pltpu.roll(x, x.shape[0] - stride, 0), x)
    return x[:rows]


def kernel(n_az, n_rad, x_in, shifts, out, *scratch):
    (x, LOW, HIGH, load_sem, A, W0, W1, O0, O1, L0, R0, L1, R1, L2, R2, state_send, state_recv, relay_send, relay_recv, gather_send, gather_recv,
     side_send, side_recv) = scratch
    fields, depth, width, lanes = x.shape
    behind = SMAX + EDGE
    whole = behind // width
    tail = behind % width
    tail_rows = -(-tail // TILE) * TILE
    group = whole + 1
    base = group * width
    first_row = width - tail_rows
    me = lax.axis_index("az")
    place = lax.rem(me, group)
    position = lax.axis_index("rad")

    def az(by):
        return {"az": lax.rem(me + by + n_az, n_az)}

    def member(by):
        return {"az": me - place + lax.rem(place + by + group, group)}

    def rad(by):
        return {"rad": position + by}

    barrier = pltpu.get_barrier_semaphore()
    MESH = pl.DeviceIdType.MESH
    load = pltpu.make_async_copy(x_in, x, load_sem)
    load.start()
    for by in (group, -group):
        pl.semaphore_signal(barrier, inc=1, device_id=az(by), device_id_type=MESH)
    for h in range(1, group):
        pl.semaphore_signal(barrier, inc=1, device_id=member(h), device_id_type=MESH)

    has_left = position > 0
    has_right = position < n_rad - 1

    @pl.when(has_left)
    def _():
        pl.semaphore_signal(barrier, inc=1, device_id=rad(-1), device_id_type=MESH)

    @pl.when(has_right)
    def _():
        pl.semaphore_signal(barrier, inc=1, device_id=rad(1), device_id_type=MESH)

    load.wait()
    A[:, :, TILE : TILE + width, :] = x[...]
    beside_me = (position + n_rad - 1) // n_rad + (2 * n_rad - 2 - position) // n_rad
    pl.semaphore_wait(barrier, group + 1 + beside_me)

    def remote(src, dst, send, recv, where):
        return pltpu.make_async_remote_copy(
            src_ref=src, dst_ref=dst, send_sem=send, recv_sem=recv, device_id=where, device_id_type=MESH
        )

    def ring_copies(z):
        pairs = []
        for side, relayed, by, rows, dst in (
            (0, LOW, 1, slice(width - TILE, width), slice(0, TILE)),
            (1, HIGH, -1, slice(0, TILE), slice(TILE + width, 2 * TILE + width)),
        ):
            own = x.at[:, z, rows]
            onward = remote(own, relayed.at[:, z], relay_send.at[side, z], relay_recv.at[side, z], az(by * group))
            sems = state_send.at[side, z], state_recv.at[side, z]
            inside = [remote(src, A.at[:, z, dst], *sems, member(by)) for src in (own, relayed.at[:, z])]
            pairs.append((place == (group - 1 if by == 1 else 0), onward, inside))
        return pairs

    def start_ring(z):
        for last, onward, inside in ring_copies(z):

            @pl.when(last)
            def _():
                onward.start()

            @pl.when(jnp.logical_not(last))
            def _():
                inside[0].start()

    def relay_ring(z):
        for last, onward, inside in ring_copies(z):

            @pl.when(last)
            def _():
                onward.wait_recv()
                inside[1].start()

    def end_ring(z):
        for last, onward, inside in ring_copies(z):
            inside[0].wait_send()

            @pl.when(last)
            def _():
                onward.wait_send()

    def side_copies(phase, src, left_dst, right_dst, z):
        to_right = remote(src.at[:, z], left_dst.at[:, z], side_send.at[phase, 0, z],
                          side_recv.at[phase, 0, z], rad(1))
        to_left = remote(src.at[:, z], right_dst.at[:, z], side_send.at[phase, 1, z],
                         side_recv.at[phase, 1, z], rad(-1))
        return to_right, to_left

    def start_side(*args):
        to_right, to_left = side_copies(*args)

        @pl.when(has_right)
        def _():
            to_right.start()

        @pl.when(has_left)
        def _():
            to_left.start()

    def await_side(*args):
        to_right, to_left = side_copies(*args)

        @pl.when(has_left)
        def _():
            to_right.wait_recv()

        @pl.when(has_right)
        def _():
            to_left.wait_recv()

    def end_side(*args):
        to_right, to_left = side_copies(*args)

        @pl.when(has_right)
        def _():
            to_right.wait_send()

        @pl.when(has_left)
        def _():
            to_left.wait_send()

    windows = (W0, W1)
    rotated = (O0, O1)
    sides = ((x, L0, R0), (O0, L1, R1), (O1, L2, R2))

    def gather_copies(step, f, z):
        W = windows[step]
        own, back = W.at[f, z, base : base + width], W.at[f, z, 0:width]
        sems = lambda h: (gather_send.at[step, h, f, z], gather_recv.at[step, h, f, z])
        onward = remote(own, back, *sems(0), az(group))
        inside = []
        for h in range(1, group):
            dst = W.at[f, z, base - h * width : base - (h - 1) * width]
            inside.append([remote(src, dst, *sems(h), member(h)) for src in (own, back)])
        return onward, inside

    def send_own(step, f, z):
        onward, inside = gather_copies(step, f, z)
        onward.start()
        for h in range(1, group):

            @pl.when(place + h < group)
            def _():
                inside[h - 1][0].start()

    def pass_on(step, f, z):
        onward, inside = gather_copies(step, f, z)
        onward.wait_recv()
        for h in range(1, group):

            @pl.when(place + h >= group)
            def _():
                inside[h - 1][1].start()

    def edges(own, left, right):
        rows = own.shape[0]
        lane = lax.broadcasted_iota(jnp.int32, (rows, lanes), 1)
        at = jnp.full((rows, lanes), position, jnp.int32)
        left = jnp.where(at == 0, jnp.broadcast_to(own[:, 0:1], own.shape), left)
        right = jnp.where(at == n_rad - 1, jnp.broadcast_to(own[:, lanes - 1 : lanes], own.shape), right)
        return jnp.where(lane < lanes // 2, right, left)

    def wide(own, beside):
        return jnp.concatenate([own, beside], axis=1)

    def hydro(step, z, strip, beside):
        rows = slice(TILE, TILE + width)
        tall = [strip(f) for f in range(fields)]
        az_speeds = face_speeds(tall[2] / tall[0], 0, COURANT_AZIMUTH)
        broad = [wide(tall[f][rows], beside(f, tall[f][rows])) for f in range(fields)]
        rad_speeds = face_speeds(broad[1] / broad[0], 1, COURANT_RADIAL)
        for f in range(fields):
            along = advect(tall[f], az_speeds, 0)[rows]
            across = advect(broad[f], rad_speeds, 1)[:, :lanes]
            windows[step][f, z, base : base + width, :] = tall[f][rows] - along - across
            send_own(step, f, z)

    def viscous(z, state, extended):
        rho, mr, mp, mz, energy = state
        own = slice(None) if extended else slice(0, lanes)
        inverse = 1.0 / rho
        pressure = (GAMMA_GAS - 1.0) * (energy - 0.5 * (mr * mr + mp * mp + mz * mz) * inverse)
        az_m, az_e = push(pressure[:, own], rho[:, own], (mp * inverse)[:, own], 0, COURANT_AZIMUTH)
        rad_m, rad_e = push(pressure, rho, mr * inverse, 1, COURANT_RADIAL)
        return [
            rho[:, own],
            mr[:, own] + rad_m[:, own],
            mp[:, own] + az_m,
            mz[:, own],
            energy[:, own] + az_e + rad_e[:, own],
        ]

    count = width + 2 * EDGE

    for z in range(depth):
        start_ring(z)
    for z in range(depth):
        start_side(0, *sides[0], z)
    for z in range(depth):
        relay_ring(z)

    for z in range(depth):
        for _, _, inside in ring_copies(z):
            inside[0].wait_recv()
        await_side(0, *sides[0], z)
        hydro(0, z, lambda f: A[f, z], lambda f, own: edges(own, L0[f, z], R0[f, z]))

    for step in range(STEPS):
        for z in range(depth):
            for f in range(fields):
                pass_on(step, f, z)
        O, L, R = sides[step + 1]
        for z in range(depth):
            for f in range(fields):
                for copies in gather_copies(step, f, z)[1]:
                    copies[0].wait_recv()
                start = base - first_row - EDGE
                O[f, z] = shifted(windows[step][f, z, first_row:], start - shifts[...], count, start - SMIN)
            start_side(step + 1, O, L, R, z)
        for z in range(depth):
            await_side(step + 1, O, L, R, z)
            state = [wide(O[f, z], edges(O[f, z], L[f, z], R[f, z])) for f in range(fields)]
            if step == STEPS - 1:
                new = viscous(z, state, False)
                for f in range(fields):
                    out[f, z] = new[f][EDGE : EDGE + width]
            else:
                new = viscous(z, state, True)
                A_rows = slice(TILE - EDGE, TILE - EDGE + count)
                for f in range(fields):
                    A[f, z, A_rows, :] = new[f][:, :lanes]
                hydro(
                    step + 1,
                    z,
                    lambda f: A[f, z],
                    lambda f, own: edges(own, *[new[f][EDGE : EDGE + width, lanes:]] * 2),
                )

    for z in range(depth):
        end_ring(z)
        for phase in range(STEPS + 1):
            end_side(phase, *sides[phase], z)
        for step in range(STEPS):
            for f in range(fields):
                onward, inside = gather_copies(step, f, z)
                onward.wait_send()
                for copies in inside:
                    copies[0].wait_send()


def body(mesh, state, shifts):
    n_az, n_rad = mesh.shape["az"], mesh.shape["rad"]
    fields, depth, width, lanes = state.shape
    behind = SMAX + EDGE
    group = behind // width + 1
    window = (group + 1) * width
    count = width + 2 * EDGE
    vmem = lambda rows: pltpu.VMEM((fields, depth, rows, lanes), jnp.float32)
    dma = pltpu.SemaphoreType.DMA
    return pl.pallas_call(
        functools.partial(kernel, n_az, n_rad),
        out_shape=pltpu.VMEM(state.shape, state.dtype),
        in_specs=[pl.BlockSpec(memory_space=pl.ANY), pl.BlockSpec(memory_space=pltpu.VMEM)],
        out_specs=pl.BlockSpec(memory_space=pltpu.VMEM),
        scratch_shapes=[
            vmem(width),
            vmem(TILE),
            vmem(TILE),
            dma(()),
            vmem(width + 2 * TILE),
            vmem(window),
            vmem(window),
            vmem(count),
            vmem(count),
            vmem(width),
            vmem(width),
            vmem(count),
            vmem(count),
            vmem(count),
            vmem(count),
            dma((2, depth)),
            dma((2, depth)),
            dma((2, depth)),
            dma((2, depth)),
            dma((STEPS, group, fields, depth)),
            dma((STEPS, group, fields, depth)),
            dma((STEPS + 1, 2, depth)),
            dma((STEPS + 1, 2, depth)),
        ],
        compiler_params=pltpu.CompilerParams(collective_id=0, has_side_effects=True),
    )(state, shifts.reshape(1, -1))


def solution(mesh):
    in_specs = (P(None, None, "az", "rad"), P("rad"))
    out_specs = P(None, None, "az", "rad")
    return jax.shard_map(
        functools.partial(body, mesh), mesh=mesh, in_specs=in_specs, out_specs=out_specs, check_vma=False
    )
```

```python
import functools

import jax
import jax.numpy as jnp
from jax import lax
from jax.experimental import pallas as pl
from jax.experimental.pallas import tpu as pltpu
from jax.sharding import PartitionSpec as P

STEPS = 2
SMIN = 4
SMAX = 96
EDGE = 4
TILE = 8

GAMMA_GAS = 1.4
COURANT_RADIAL = 0.15
COURANT_AZIMUTH = 0.15
VISCOSITY_COEF = 1.0


def up(x, axis):
    return pltpu.roll(x, x.shape[axis] - 1, axis)


def down(x, axis):
    return pltpu.roll(x, 1, axis)


def face_speeds(velocity, axis, courant):
    face = (0.5 * courant) * (velocity + up(velocity, axis))
    return jnp.maximum(face, 0.0), jnp.minimum(face, 0.0)


def advect(field, speeds, axis):
    low = field - down(field, axis)
    high = up(low, axis)
    product = low * high
    positive = product > 0
    half = jnp.where(positive, product / jnp.where(positive, low + high, 1.0), 0.0)
    flux = speeds[0] * (field + half) + speeds[1] * up(field - half, axis)
    return flux - down(flux, axis)


def push(pressure, density, speed, axis, courant):
    compress = jnp.minimum(up(speed, axis) - down(speed, axis), 0.0)
    total = pressure + VISCOSITY_COEF * density * compress * compress
    work = total * speed
    scale = -0.5 * courant
    return scale * (up(total, axis) - down(total, axis)), scale * (up(work, axis) - down(work, axis))


def shifted(window, shift_left, rows, longest):
    bits = longest.bit_length()
    x = window
    for bit in reversed(range(bits)):
        stride = 1 << bit
        left = stride - 1
        if stride >= TILE:
            keep = -(-(rows + left) // TILE) * TILE
            chosen = min(keep, x.shape[0] - stride)
            mask = (jnp.broadcast_to(shift_left, (chosen, shift_left.shape[1])) & stride) != 0
            y = jnp.where(mask, x[stride : stride + chosen], x[:chosen])
            x = y if chosen == keep else jnp.concatenate([y, x[chosen:keep]], axis=0)
        else:
            mask = (jnp.broadcast_to(shift_left, x.shape) & stride) != 0
            x = jnp.where(mask, pltpu.roll(x, x.shape[0] - stride, 0), x)
    return x[:rows]


def kernel(n_az, n_rad, x_in, shifts, out, *scratch):
    (x, LOW, HIGH, load_sem, A, W0, W1, O0, O1, L0, R0, L1, R1, L2, R2, state_send, state_recv, relay_send, relay_recv, gather_send, gather_recv,
     side_send, side_recv) = scratch
    fields, depth, width, lanes = x.shape
    behind = SMAX + EDGE
    whole = behind // width
    tail = behind % width
    tail_rows = -(-tail // TILE) * TILE
    group = whole + 1
    base = group * width
    first_row = width - tail_rows
    me = lax.axis_index("az")
    place = lax.rem(me, group)
    position = lax.axis_index("rad")

    def az(by):
        return {"az": lax.rem(me + by + n_az, n_az)}

    def member(by):
        return {"az": me - place + lax.rem(place + by + group, group)}

    def rad(by):
        return {"rad": position + by}

    barrier = pltpu.get_barrier_semaphore()
    MESH = pl.DeviceIdType.MESH
    load = pltpu.make_async_copy(x_in, x, load_sem)
    load.start()
    for by in (group, -group):
        pl.semaphore_signal(barrier, inc=1, device_id=az(by), device_id_type=MESH)
    for h in range(1, group):
        pl.semaphore_signal(barrier, inc=1, device_id=member(h), device_id_type=MESH)

    has_left = position > 0
    has_right = position < n_rad - 1

    @pl.when(has_left)
    def _():
        pl.semaphore_signal(barrier, inc=1, device_id=rad(-1), device_id_type=MESH)

    @pl.when(has_right)
    def _():
        pl.semaphore_signal(barrier, inc=1, device_id=rad(1), device_id_type=MESH)

    load.wait()
    A[:, :, TILE : TILE + width, :] = x[...]
    beside_me = (position + n_rad - 1) // n_rad + (2 * n_rad - 2 - position) // n_rad
    pl.semaphore_wait(barrier, group + 1 + beside_me)

    def remote(src, dst, send, recv, where):
        return pltpu.make_async_remote_copy(
            src_ref=src, dst_ref=dst, send_sem=send, recv_sem=recv, device_id=where, device_id_type=MESH
        )

    def ring_copies(z):
        pairs = []
        for side, relayed, by, rows, dst in (
            (0, LOW, 1, slice(width - TILE, width), slice(0, TILE)),
            (1, HIGH, -1, slice(0, TILE), slice(TILE + width, 2 * TILE + width)),
        ):
            own = x.at[:, z, rows]
            onward = remote(own, relayed.at[:, z], relay_send.at[side, z], relay_recv.at[side, z], az(by * group))
            sems = state_send.at[side, z], state_recv.at[side, z]
            inside = [remote(src, A.at[:, z, dst], *sems, member(by)) for src in (own, relayed.at[:, z])]
            pairs.append((place == (group - 1 if by == 1 else 0), onward, inside))
        return pairs

    def start_ring(z):
        for last, onward, inside in ring_copies(z):

            @pl.when(last)
            def _():
                onward.start()

            @pl.when(jnp.logical_not(last))
            def _():
                inside[0].start()

    def relay_ring(z):
        for last, onward, inside in ring_copies(z):

            @pl.when(last)
            def _():
                onward.wait_recv()
                inside[1].start()

    def end_ring(z):
        for last, onward, inside in ring_copies(z):
            inside[0].wait_send()

            @pl.when(last)
            def _():
                onward.wait_send()

    def side_copies(phase, src, left_dst, right_dst, z):
        to_right = remote(src.at[:, z], left_dst.at[:, z], side_send.at[phase, 0, z],
                          side_recv.at[phase, 0, z], rad(1))
        to_left = remote(src.at[:, z], right_dst.at[:, z], side_send.at[phase, 1, z],
                         side_recv.at[phase, 1, z], rad(-1))
        return to_right, to_left

    def start_side(*args):
        to_right, to_left = side_copies(*args)

        @pl.when(has_right)
        def _():
            to_right.start()

        @pl.when(has_left)
        def _():
            to_left.start()

    def await_side(*args):
        to_right, to_left = side_copies(*args)

        @pl.when(has_left)
        def _():
            to_right.wait_recv()

        @pl.when(has_right)
        def _():
            to_left.wait_recv()

    def end_side(*args):
        to_right, to_left = side_copies(*args)

        @pl.when(has_right)
        def _():
            to_right.wait_send()

        @pl.when(has_left)
        def _():
            to_left.wait_send()

    windows = (W0, W1)
    parts = (((TILE, width - 2 * TILE), (0, TILE), (width - TILE, TILE)), ((0, width),))
    rotated = (O0, O1)
    sides = ((x, L0, R0), (O0, L1, R1), (O1, L2, R2))

    def gather_copies(step, part, f, z):
        W = windows[step]
        first, rows = parts[step][part]
        if step == 0 and part > 0:
            f, slot = slice(None), 0
        else:
            slot = f
        own, back = W.at[f, z, base + first : base + first + rows], W.at[f, z, first : first + rows]
        index = lambda h: (step + part if step == 0 else STEPS + 1, h, slot, z)
        sems = lambda h: (gather_send.at[index(h)], gather_recv.at[index(h)])
        onward = remote(own, back, *sems(0), az(group))
        inside = []
        for h in range(1, group):
            start = base - h * width + first
            dst = W.at[f, z, start : start + rows]
            inside.append([remote(src, dst, *sems(h), member(h)) for src in (own, back)])
        return onward, inside

    def send_own(*which):
        onward, inside = gather_copies(*which)
        onward.start()
        for h in range(1, group):

            @pl.when(place + h < group)
            def _():
                inside[h - 1][0].start()

    def pass_on(*which):
        onward, inside = gather_copies(*which)
        onward.wait_recv()
        for h in range(1, group):

            @pl.when(place + h >= group)
            def _():
                inside[h - 1][1].start()

    def await_group(*which):
        for copies in gather_copies(*which)[1]:
            copies[0].wait_recv()

    def edges(own, left, right):
        rows = own.shape[0]
        lane = lax.broadcasted_iota(jnp.int32, (rows, lanes), 1)
        at = jnp.full((rows, lanes), position, jnp.int32)
        left = jnp.where(at == 0, jnp.broadcast_to(own[:, 0:1], own.shape), left)
        right = jnp.where(at == n_rad - 1, jnp.broadcast_to(own[:, lanes - 1 : lanes], own.shape), right)
        return jnp.where(lane < lanes // 2, right, left)

    def wide(own, beside):
        return jnp.concatenate([own, beside], axis=1)

    def hydro(step, z, strip, beside, which):
        inner = step == 0 and which[0] == 0
        rows = slice(0, width) if inner else slice(TILE, TILE + width)
        tall = [strip(f) for f in range(fields)]
        az_speeds = face_speeds(tall[2] / tall[0], 0, COURANT_AZIMUTH)
        broad = [wide(tall[f][rows], beside(f, tall[f][rows])) for f in range(fields)]
        rad_speeds = face_speeds(broad[1] / broad[0], 1, COURANT_RADIAL)
        for f in range(fields):
            along = advect(tall[f], az_speeds, 0)[rows]
            across = advect(broad[f], rad_speeds, 1)[:, :lanes]
            new = tall[f][rows] - along - across
            for part in which:
                first, height = parts[step][part]
                windows[step][f, z, base + first : base + first + height, :] = new[first : first + height]
            if which[0] == 0:
                send_own(step, 0, f, z)
        if which[0] > 0:
            for part in which:
                send_own(step, part, 0, z)

    def viscous(z, state, extended):
        rho, mr, mp, mz, energy = state
        own = slice(None) if extended else slice(0, lanes)
        inverse = 1.0 / rho
        pressure = (GAMMA_GAS - 1.0) * (energy - 0.5 * (mr * mr + mp * mp + mz * mz) * inverse)
        az_m, az_e = push(pressure[:, own], rho[:, own], (mp * inverse)[:, own], 0, COURANT_AZIMUTH)
        rad_m, rad_e = push(pressure, rho, mr * inverse, 1, COURANT_RADIAL)
        return [
            rho[:, own],
            mr[:, own] + rad_m[:, own],
            mp[:, own] + az_m,
            mz[:, own],
            energy[:, own] + az_e + rad_e[:, own],
        ]

    count = width + 2 * EDGE

    for z in range(depth):
        start_ring(z)
    for z in range(depth):
        start_side(0, *sides[0], z)
    def first_hydro(z, which):
        strip = (lambda f: x[f, z]) if which[0] == 0 else (lambda f: A[f, z])
        hydro(0, z, strip, lambda f, own: edges(own, L0[f, z], R0[f, z]), which)

    for z in range(depth):
        await_side(0, *sides[0], z)
        first_hydro(z, (0,))
    for z in range(depth):
        relay_ring(z)
    for z in range(depth):
        for _, _, inside in ring_copies(z):
            inside[0].wait_recv()
        first_hydro(z, (1, 2))

    for step in range(STEPS):
        for z in range(depth):
            for f in range(fields):
                pass_on(step, 0, f, z)
        for z in range(depth):
            for part in range(1, len(parts[step])):
                pass_on(step, part, 0, z)
        O, L, R = sides[step + 1]
        for z in range(depth):
            for part in range(1, len(parts[step])):
                await_group(step, part, 0, z)
            for f in range(fields):
                await_group(step, 0, f, z)
                start = base - first_row - EDGE
                O[f, z] = shifted(windows[step][f, z, first_row:], start - shifts[...], count, start - SMIN)
            start_side(step + 1, O, L, R, z)
        for z in range(depth):
            await_side(step + 1, O, L, R, z)
            state = [wide(O[f, z], edges(O[f, z], L[f, z], R[f, z])) for f in range(fields)]
            if step == STEPS - 1:
                new = viscous(z, state, False)
                for f in range(fields):
                    out[f, z] = new[f][EDGE : EDGE + width]
            else:
                new = viscous(z, state, True)
                A_rows = slice(TILE - EDGE, TILE - EDGE + count)
                for f in range(fields):
                    A[f, z, A_rows, :] = new[f][:, :lanes]
                hydro(
                    step + 1,
                    z,
                    lambda f: A[f, z],
                    lambda f, own: edges(own, *[new[f][EDGE : EDGE + width, lanes:]] * 2),
                    (0,),
                )

    for z in range(depth):
        end_ring(z)
        for phase in range(STEPS + 1):
            end_side(phase, *sides[phase], z)
        for step in range(STEPS):
            for part in range(len(parts[step])):
                for f in range(fields if part == 0 else 1):
                    onward, inside = gather_copies(step, part, f, z)
                    onward.wait_send()
                    for copies in inside:
                        copies[0].wait_send()


def body(mesh, state, shifts):
    n_az, n_rad = mesh.shape["az"], mesh.shape["rad"]
    fields, depth, width, lanes = state.shape
    behind = SMAX + EDGE
    group = behind // width + 1
    window = (group + 1) * width
    count = width + 2 * EDGE
    vmem = lambda rows: pltpu.VMEM((fields, depth, rows, lanes), jnp.float32)
    dma = pltpu.SemaphoreType.DMA
    return pl.pallas_call(
        functools.partial(kernel, n_az, n_rad),
        out_shape=pltpu.VMEM(state.shape, state.dtype),
        in_specs=[pl.BlockSpec(memory_space=pl.ANY), pl.BlockSpec(memory_space=pltpu.VMEM)],
        out_specs=pl.BlockSpec(memory_space=pltpu.VMEM),
        scratch_shapes=[
            vmem(width),
            vmem(TILE),
            vmem(TILE),
            dma(()),
            vmem(width + 2 * TILE),
            vmem(window),
            vmem(window),
            vmem(count),
            vmem(count),
            vmem(width),
            vmem(width),
            vmem(count),
            vmem(count),
            vmem(count),
            vmem(count),
            dma((2, depth)),
            dma((2, depth)),
            dma((2, depth)),
            dma((2, depth)),
            dma((STEPS + 2, group, fields, depth)),
            dma((STEPS + 2, group, fields, depth)),
            dma((STEPS + 1, 2, depth)),
            dma((STEPS + 1, 2, depth)),
        ],
        compiler_params=pltpu.CompilerParams(collective_id=0, has_side_effects=True),
    )(state, shifts.reshape(1, -1))


def solution(mesh):
    in_specs = (P(None, None, "az", "rad"), P("rad"))
    out_specs = P(None, None, "az", "rad")
    return jax.shard_map(
        functools.partial(body, mesh), mesh=mesh, in_specs=in_specs, out_specs=out_specs, check_vma=False
    )
```

```python
import functools

import jax
import jax.numpy as jnp
from jax import lax
from jax.experimental import pallas as pl
from jax.experimental.pallas import tpu as pltpu
from jax.sharding import PartitionSpec as P

STEPS = 2
SMIN = 4
SMAX = 96
EDGE = 4
TILE = 8

GAMMA_GAS = 1.4
COURANT_RADIAL = 0.15
COURANT_AZIMUTH = 0.15
VISCOSITY_COEF = 1.0


def up(x, axis):
    return pltpu.roll(x, x.shape[axis] - 1, axis)


def down(x, axis):
    return pltpu.roll(x, 1, axis)


def face_speeds(velocity, axis, courant):
    face = (0.5 * courant) * (velocity + up(velocity, axis))
    return jnp.maximum(face, 0.0), jnp.minimum(face, 0.0)


def advect(field, speeds, axis):
    low = field - down(field, axis)
    high = up(low, axis)
    product = low * high
    positive = product > 0
    half = jnp.where(positive, product / jnp.where(positive, low + high, 1.0), 0.0)
    flux = speeds[0] * (field + half) + speeds[1] * up(field - half, axis)
    return flux - down(flux, axis)


def push(pressure, density, speed, axis, courant):
    compress = jnp.minimum(up(speed, axis) - down(speed, axis), 0.0)
    total = pressure + VISCOSITY_COEF * density * compress * compress
    work = total * speed
    scale = -0.5 * courant
    return scale * (up(total, axis) - down(total, axis)), scale * (up(work, axis) - down(work, axis))


def shifted(window, shift_left, rows, longest):
    bits = longest.bit_length()
    x = window
    for bit in reversed(range(bits)):
        stride = 1 << bit
        left = stride - 1
        if stride >= TILE:
            keep = -(-(rows + left) // TILE) * TILE
            chosen = min(keep, x.shape[0] - stride)
            mask = (jnp.broadcast_to(shift_left, (chosen, shift_left.shape[1])) & stride) != 0
            y = jnp.where(mask, x[stride : stride + chosen], x[:chosen])
            x = y if chosen == keep else jnp.concatenate([y, x[chosen:keep]], axis=0)
        else:
            mask = (jnp.broadcast_to(shift_left, x.shape) & stride) != 0
            x = jnp.where(mask, pltpu.roll(x, x.shape[0] - stride, 0), x)
    return x[:rows]


def kernel(n_az, n_rad, x_in, shifts, out, *scratch):
    (x, LOW, HIGH, load_sem, A, W0, W1, O0, O1, L0, R0, L1, R1, L2, R2, state_send, state_recv, relay_send, relay_recv, gather_send, gather_recv,
     side_send, side_recv) = scratch
    fields, depth, width, lanes = x.shape
    behind = SMAX + EDGE
    whole = behind // width
    tail = behind % width
    tail_rows = -(-tail // TILE) * TILE
    group = whole + 1
    base = group * width
    first_row = width - tail_rows
    me = lax.axis_index("az")
    place = lax.rem(me, group)
    position = lax.axis_index("rad")

    def az(by):
        return {"az": lax.rem(me + by + n_az, n_az)}

    def member(by):
        return {"az": me - place + lax.rem(place + by + group, group)}

    def rad(by):
        return {"rad": position + by}

    barrier = pltpu.get_barrier_semaphore()
    MESH = pl.DeviceIdType.MESH
    load = pltpu.make_async_copy(x_in, x, load_sem)
    load.start()
    for by in (group, -group):
        pl.semaphore_signal(barrier, inc=1, device_id=az(by), device_id_type=MESH)
    for h in range(1, group):
        pl.semaphore_signal(barrier, inc=1, device_id=member(h), device_id_type=MESH)

    has_left = position > 0
    has_right = position < n_rad - 1

    @pl.when(has_left)
    def _():
        pl.semaphore_signal(barrier, inc=1, device_id=rad(-1), device_id_type=MESH)

    @pl.when(has_right)
    def _():
        pl.semaphore_signal(barrier, inc=1, device_id=rad(1), device_id_type=MESH)

    load.wait()
    A[:, :, TILE : TILE + width, :] = x[...]
    beside_me = (position + n_rad - 1) // n_rad + (2 * n_rad - 2 - position) // n_rad
    pl.semaphore_wait(barrier, group + 1 + beside_me)

    def remote(src, dst, send, recv, where):
        return pltpu.make_async_remote_copy(
            src_ref=src, dst_ref=dst, send_sem=send, recv_sem=recv, device_id=where, device_id_type=MESH
        )

    def ring_copies(z):
        pairs = []
        for side, relayed, by, rows, dst in (
            (0, LOW, 1, slice(width - TILE, width), slice(0, TILE)),
            (1, HIGH, -1, slice(0, TILE), slice(TILE + width, 2 * TILE + width)),
        ):
            own = x.at[:, z, rows]
            onward = remote(own, relayed.at[:, z], relay_send.at[side, z], relay_recv.at[side, z], az(by * group))
            sems = state_send.at[side, z], state_recv.at[side, z]
            inside = [remote(src, A.at[:, z, dst], *sems, member(by)) for src in (own, relayed.at[:, z])]
            pairs.append((place == (group - 1 if by == 1 else 0), onward, inside))
        return pairs

    def start_ring(z):
        for last, onward, inside in ring_copies(z):

            @pl.when(last)
            def _():
                onward.start()

            @pl.when(jnp.logical_not(last))
            def _():
                inside[0].start()

    def relay_ring(z):
        for last, onward, inside in ring_copies(z):

            @pl.when(last)
            def _():
                onward.wait_recv()
                inside[1].start()

    def end_ring(z):
        for last, onward, inside in ring_copies(z):
            inside[0].wait_send()

            @pl.when(last)
            def _():
                onward.wait_send()

    def side_copies(phase, src, left_dst, right_dst, z):
        to_right = remote(src.at[:, z], left_dst.at[:, z], side_send.at[phase, 0, z],
                          side_recv.at[phase, 0, z], rad(1))
        to_left = remote(src.at[:, z], right_dst.at[:, z], side_send.at[phase, 1, z],
                         side_recv.at[phase, 1, z], rad(-1))
        return to_right, to_left

    def start_side(*args):
        to_right, to_left = side_copies(*args)

        @pl.when(has_right)
        def _():
            to_right.start()

        @pl.when(has_left)
        def _():
            to_left.start()

    def await_side(*args):
        to_right, to_left = side_copies(*args)

        @pl.when(has_left)
        def _():
            to_right.wait_recv()

        @pl.when(has_right)
        def _():
            to_left.wait_recv()

    def end_side(*args):
        to_right, to_left = side_copies(*args)

        @pl.when(has_right)
        def _():
            to_right.wait_send()

        @pl.when(has_left)
        def _():
            to_left.wait_send()

    windows = (W0, W1)
    parts = (((TILE, width - 2 * TILE), (0, TILE), (width - TILE, TILE)), ((0, width),))
    rotated = (O0, O1)
    sides = ((x, L0, R0), (O0, L1, R1), (O1, L2, R2))

    def gather_copies(step, part, f, z):
        W = windows[step]
        first, rows = parts[step][part]
        if step == 0 and part > 0:
            f, slot = slice(None), 0
        else:
            slot = f
        own, back = W.at[f, z, base + first : base + first + rows], W.at[f, z, first : first + rows]
        index = lambda h: (step + part if step == 0 else STEPS + 1, h, slot, z)
        sems = lambda h: (gather_send.at[index(h)], gather_recv.at[index(h)])
        onward = remote(own, back, *sems(0), az(group))
        inside = []
        for h in range(1, group):
            start = base - h * width + first
            dst = W.at[f, z, start : start + rows]
            inside.append([remote(src, dst, *sems(h), member(h)) for src in (own, back)])
        return onward, inside

    def send_own(*which):
        onward, inside = gather_copies(*which)
        onward.start()
        for h in range(1, group):

            @pl.when(place + h < group)
            def _():
                inside[h - 1][0].start()

    def pass_on(*which):
        onward, inside = gather_copies(*which)
        onward.wait_recv()
        for h in range(1, group):

            @pl.when(place + h >= group)
            def _():
                inside[h - 1][1].start()

    def await_group(*which):
        for copies in gather_copies(*which)[1]:
            copies[0].wait_recv()

    def edges(own, left, right):
        rows = own.shape[0]
        lane = lax.broadcasted_iota(jnp.int32, (rows, lanes), 1)
        at = jnp.full((rows, lanes), position, jnp.int32)
        left = jnp.where(at == 0, jnp.broadcast_to(own[:, 0:1], own.shape), left)
        right = jnp.where(at == n_rad - 1, jnp.broadcast_to(own[:, lanes - 1 : lanes], own.shape), right)
        return jnp.where(lane < lanes // 2, right, left)

    def wide(own, beside):
        return jnp.concatenate([own, beside], axis=1)

    def hydro(step, z, strip, beside, which):
        inner = step == 0 and which[0] == 0
        rows = slice(0, width) if inner else slice(TILE, TILE + width)
        tall = [strip(f) for f in range(fields)]
        az_speeds = face_speeds(tall[2] / tall[0], 0, COURANT_AZIMUTH)
        broad = [wide(tall[f][rows], beside(f, tall[f][rows])) for f in range(fields)]
        rad_speeds = face_speeds(broad[1] / broad[0], 1, COURANT_RADIAL)
        for f in range(fields):
            along = advect(tall[f], az_speeds, 0)[rows]
            across = advect(broad[f], rad_speeds, 1)[:, :lanes]
            new = tall[f][rows] - along - across
            for part in which:
                first, height = parts[step][part]
                windows[step][f, z, base + first : base + first + height, :] = new[first : first + height]
            if which[0] == 0:
                send_own(step, 0, f, z)
        if which[0] > 0:
            for part in which:
                send_own(step, part, 0, z)

    def viscous(z, state, extended):
        rho, mr, mp, mz, energy = state
        own = slice(None) if extended else slice(0, lanes)
        inverse = 1.0 / rho
        pressure = (GAMMA_GAS - 1.0) * (energy - 0.5 * (mr * mr + mp * mp + mz * mz) * inverse)
        az_m, az_e = push(pressure[:, own], rho[:, own], (mp * inverse)[:, own], 0, COURANT_AZIMUTH)
        rad_m, rad_e = push(pressure, rho, mr * inverse, 1, COURANT_RADIAL)
        return [
            rho[:, own],
            mr[:, own] + rad_m[:, own],
            mp[:, own] + az_m,
            mz[:, own],
            energy[:, own] + az_e + rad_e[:, own],
        ]

    count = width + 2 * EDGE

    for z in range(depth):
        start_ring(z)
    for z in range(depth):
        start_side(0, *sides[0], z)
    def first_hydro(z, which):
        strip = (lambda f: x[f, z]) if which[0] == 0 else (lambda f: A[f, z])
        hydro(0, z, strip, lambda f, own: edges(own, L0[f, z], R0[f, z]), which)

    for z in range(depth):
        relay_ring(z)
    for z in range(depth):
        await_side(0, *sides[0], z)
        first_hydro(z, (0,))
    for z in range(depth):
        for _, _, inside in ring_copies(z):
            inside[0].wait_recv()
        first_hydro(z, (1, 2))

    for step in range(STEPS):
        for z in range(depth):
            for f in range(fields):
                pass_on(step, 0, f, z)
        for z in range(depth):
            for part in range(1, len(parts[step])):
                pass_on(step, part, 0, z)
        O, L, R = sides[step + 1]
        for z in range(depth):
            for part in range(1, len(parts[step])):
                await_group(step, part, 0, z)
            for f in range(fields):
                await_group(step, 0, f, z)
                start = base - first_row - EDGE
                O[f, z] = shifted(windows[step][f, z, first_row:], start - shifts[...], count, start - SMIN)
            start_side(step + 1, O, L, R, z)
        for z in range(depth):
            await_side(step + 1, O, L, R, z)
            state = [wide(O[f, z], edges(O[f, z], L[f, z], R[f, z])) for f in range(fields)]
            if step == STEPS - 1:
                new = viscous(z, state, False)
                for f in range(fields):
                    out[f, z] = new[f][EDGE : EDGE + width]
            else:
                new = viscous(z, state, True)
                A_rows = slice(TILE - EDGE, TILE - EDGE + count)
                for f in range(fields):
                    A[f, z, A_rows, :] = new[f][:, :lanes]
                hydro(
                    step + 1,
                    z,
                    lambda f: A[f, z],
                    lambda f, own: edges(own, *[new[f][EDGE : EDGE + width, lanes:]] * 2),
                    (0,),
                )

    for z in range(depth):
        end_ring(z)
        for phase in range(STEPS + 1):
            end_side(phase, *sides[phase], z)
        for step in range(STEPS):
            for part in range(len(parts[step])):
                for f in range(fields if part == 0 else 1):
                    onward, inside = gather_copies(step, part, f, z)
                    onward.wait_send()
                    for copies in inside:
                        copies[0].wait_send()


def body(mesh, state, shifts):
    n_az, n_rad = mesh.shape["az"], mesh.shape["rad"]
    fields, depth, width, lanes = state.shape
    behind = SMAX + EDGE
    group = behind // width + 1
    window = (group + 1) * width
    count = width + 2 * EDGE
    vmem = lambda rows: pltpu.VMEM((fields, depth, rows, lanes), jnp.float32)
    dma = pltpu.SemaphoreType.DMA
    return pl.pallas_call(
        functools.partial(kernel, n_az, n_rad),
        out_shape=pltpu.VMEM(state.shape, state.dtype),
        in_specs=[pl.BlockSpec(memory_space=pl.ANY), pl.BlockSpec(memory_space=pltpu.VMEM)],
        out_specs=pl.BlockSpec(memory_space=pltpu.VMEM),
        scratch_shapes=[
            vmem(width),
            vmem(TILE),
            vmem(TILE),
            dma(()),
            vmem(width + 2 * TILE),
            vmem(window),
            vmem(window),
            vmem(count),
            vmem(count),
            vmem(width),
            vmem(width),
            vmem(count),
            vmem(count),
            vmem(count),
            vmem(count),
            dma((2, depth)),
            dma((2, depth)),
            dma((2, depth)),
            dma((2, depth)),
            dma((STEPS + 2, group, fields, depth)),
            dma((STEPS + 2, group, fields, depth)),
            dma((STEPS + 1, 2, depth)),
            dma((STEPS + 1, 2, depth)),
        ],
        compiler_params=pltpu.CompilerParams(collective_id=0, has_side_effects=True),
    )(state, shifts.reshape(1, -1))


def solution(mesh):
    in_specs = (P(None, None, "az", "rad"), P("rad"))
    out_specs = P(None, None, "az", "rad")
    return jax.shard_map(
        functools.partial(body, mesh), mesh=mesh, in_specs=in_specs, out_specs=out_specs, check_vma=False
    )
```

```python
import functools

import jax
import jax.numpy as jnp
from jax import lax
from jax.experimental import pallas as pl
from jax.experimental.pallas import tpu as pltpu
from jax.sharding import PartitionSpec as P

STEPS = 2
SMIN = 4
SMAX = 96
EDGE = 4
TILE = 8

GAMMA_GAS = 1.4
COURANT_RADIAL = 0.15
COURANT_AZIMUTH = 0.15
VISCOSITY_COEF = 1.0


def up(x, axis):
    return pltpu.roll(x, x.shape[axis] - 1, axis)


def down(x, axis):
    return pltpu.roll(x, 1, axis)


def face_speeds(velocity, axis, courant):
    face = (0.5 * courant) * (velocity + up(velocity, axis))
    return jnp.maximum(face, 0.0), jnp.minimum(face, 0.0)


def advect(field, speeds, axis):
    low = field - down(field, axis)
    high = up(low, axis)
    product = low * high
    positive = product > 0
    half = jnp.where(positive, product / jnp.where(positive, low + high, 1.0), 0.0)
    flux = speeds[0] * (field + half) + speeds[1] * up(field - half, axis)
    return flux - down(flux, axis)


def push(pressure, density, speed, axis, courant):
    compress = jnp.minimum(up(speed, axis) - down(speed, axis), 0.0)
    total = pressure + VISCOSITY_COEF * density * compress * compress
    work = total * speed
    scale = -0.5 * courant
    return scale * (up(total, axis) - down(total, axis)), scale * (up(work, axis) - down(work, axis))


def shifted(window, shift_left, rows, longest):
    bits = longest.bit_length()
    x = window
    for bit in reversed(range(bits)):
        stride = 1 << bit
        left = stride - 1
        if stride >= TILE:
            keep = -(-(rows + left) // TILE) * TILE
            chosen = min(keep, x.shape[0] - stride)
            mask = (jnp.broadcast_to(shift_left, (chosen, shift_left.shape[1])) & stride) != 0
            y = jnp.where(mask, x[stride : stride + chosen], x[:chosen])
            x = y if chosen == keep else jnp.concatenate([y, x[chosen:keep]], axis=0)
        else:
            mask = (jnp.broadcast_to(shift_left, x.shape) & stride) != 0
            x = jnp.where(mask, pltpu.roll(x, x.shape[0] - stride, 0), x)
    return x[:rows]


def kernel(n_az, n_rad, x_in, shifts, out, *scratch):
    (x, load_sem, A, W0, W1, O0, O1, L0, R0, L1, R1, L2, R2, state_send, state_recv, gather_send, gather_recv,
     side_send, side_recv) = scratch
    fields, depth, width, lanes = x.shape
    behind = SMAX + EDGE
    whole = behind // width
    tail = behind % width
    tail_rows = -(-tail // TILE) * TILE
    group = whole + 1
    base = group * width
    first_row = width - tail_rows
    me = lax.axis_index("az")
    place = lax.rem(me, group)
    position = lax.axis_index("rad")

    def az(by):
        return {"az": lax.rem(me + by + n_az, n_az)}

    def member(by):
        return {"az": me - place + lax.rem(place + by + group, group)}

    def rad(by):
        return {"rad": position + by}

    barrier = pltpu.get_barrier_semaphore()
    MESH = pl.DeviceIdType.MESH
    load = pltpu.make_async_copy(x_in, x, load_sem)
    load.start()
    for by in (1, -1, -group):
        pl.semaphore_signal(barrier, inc=1, device_id=az(by), device_id_type=MESH)
    for h in range(1, group):
        pl.semaphore_signal(barrier, inc=1, device_id=member(h), device_id_type=MESH)

    has_left = position > 0
    has_right = position < n_rad - 1

    @pl.when(has_left)
    def _():
        pl.semaphore_signal(barrier, inc=1, device_id=rad(-1), device_id_type=MESH)

    @pl.when(has_right)
    def _():
        pl.semaphore_signal(barrier, inc=1, device_id=rad(1), device_id_type=MESH)

    load.wait()
    A[:, :, TILE : TILE + width, :] = x[...]
    beside_me = (position + n_rad - 1) // n_rad + (2 * n_rad - 2 - position) // n_rad
    pl.semaphore_wait(barrier, group + 2 + beside_me)

    def remote(src, dst, send, recv, where):
        return pltpu.make_async_remote_copy(
            src_ref=src, dst_ref=dst, send_sem=send, recv_sem=recv, device_id=where, device_id_type=MESH
        )

    def ring_copies(z):
        return [
            remote(x.at[:, z, width - TILE : width], A.at[:, z, 0:TILE],
                   state_send.at[0, z], state_recv.at[0, z], az(1)),
            remote(x.at[:, z, 0:TILE], A.at[:, z, TILE + width : 2 * TILE + width],
                   state_send.at[1, z], state_recv.at[1, z], az(-1)),
        ]

    def side_copies(phase, src, left_dst, right_dst, z):
        to_right = remote(src.at[:, z], left_dst.at[:, z], side_send.at[phase, 0, z],
                          side_recv.at[phase, 0, z], rad(1))
        to_left = remote(src.at[:, z], right_dst.at[:, z], side_send.at[phase, 1, z],
                         side_recv.at[phase, 1, z], rad(-1))
        return to_right, to_left

    def start_side(*args):
        to_right, to_left = side_copies(*args)

        @pl.when(has_right)
        def _():
            to_right.start()

        @pl.when(has_left)
        def _():
            to_left.start()

    def await_side(*args):
        to_right, to_left = side_copies(*args)

        @pl.when(has_left)
        def _():
            to_right.wait_recv()

        @pl.when(has_right)
        def _():
            to_left.wait_recv()

    def end_side(*args):
        to_right, to_left = side_copies(*args)

        @pl.when(has_right)
        def _():
            to_right.wait_send()

        @pl.when(has_left)
        def _():
            to_left.wait_send()

    windows = (W0, W1)
    rotated = (O0, O1)
    sides = ((x, L0, R0), (O0, L1, R1), (O1, L2, R2))

    def gather_copies(step, f, z):
        W = windows[step]
        own, back = W.at[f, z, base : base + width], W.at[f, z, 0:width]
        sems = lambda h: (gather_send.at[step, h, f, z], gather_recv.at[step, h, f, z])
        onward = remote(own, back, *sems(0), az(group))
        inside = []
        for h in range(1, group):
            dst = W.at[f, z, base - h * width : base - (h - 1) * width]
            inside.append([remote(src, dst, *sems(h), member(h)) for src in (own, back)])
        return onward, inside

    def send_own(step, f, z):
        onward, inside = gather_copies(step, f, z)
        onward.start()
        for h in range(1, group):

            @pl.when(place + h < group)
            def _():
                inside[h - 1][0].start()

    def pass_on(step, f, z):
        onward, inside = gather_copies(step, f, z)
        onward.wait_recv()
        for h in range(1, group):

            @pl.when(place + h >= group)
            def _():
                inside[h - 1][1].start()

    def edges(own, left, right):
        rows = own.shape[0]
        lane = lax.broadcasted_iota(jnp.int32, (rows, lanes), 1)
        at = jnp.full((rows, lanes), position, jnp.int32)
        left = jnp.where(at == 0, jnp.broadcast_to(own[:, 0:1], own.shape), left)
        right = jnp.where(at == n_rad - 1, jnp.broadcast_to(own[:, lanes - 1 : lanes], own.shape), right)
        return jnp.where(lane < lanes // 2, right, left)

    def wide(own, beside):
        return jnp.concatenate([own, beside], axis=1)

    def hydro(step, z, strip, beside):
        rows = slice(TILE, TILE + width)
        tall = [strip(f) for f in range(fields)]
        az_speeds = face_speeds(tall[2] / tall[0], 0, COURANT_AZIMUTH)
        broad = [wide(tall[f][rows], beside(f, tall[f][rows])) for f in range(fields)]
        rad_speeds = face_speeds(broad[1] / broad[0], 1, COURANT_RADIAL)
        for f in range(fields):
            along = advect(tall[f], az_speeds, 0)[rows]
            across = advect(broad[f], rad_speeds, 1)[:, :lanes]
            windows[step][f, z, base : base + width, :] = tall[f][rows] - along - across
            send_own(step, f, z)

    def viscous(z, state, extended):
        rho, mr, mp, mz, energy = state
        own = slice(None) if extended else slice(0, lanes)
        inverse = 1.0 / rho
        pressure = (GAMMA_GAS - 1.0) * (energy - 0.5 * (mr * mr + mp * mp + mz * mz) * inverse)
        az_m, az_e = push(pressure[:, own], rho[:, own], (mp * inverse)[:, own], 0, COURANT_AZIMUTH)
        rad_m, rad_e = push(pressure, rho, mr * inverse, 1, COURANT_RADIAL)
        return [
            rho[:, own],
            mr[:, own] + rad_m[:, own],
            mp[:, own] + az_m,
            mz[:, own],
            energy[:, own] + az_e + rad_e[:, own],
        ]

    count = width + 2 * EDGE

    for z in range(depth):
        for copy in ring_copies(z):
            copy.start()
    for z in range(depth):
        start_side(0, *sides[0], z)
    for z in range(depth):
        for copy in ring_copies(z):
            copy.wait_recv()
        await_side(0, *sides[0], z)
        hydro(0, z, lambda f: A[f, z], lambda f, own: edges(own, L0[f, z], R0[f, z]))

    for step in range(STEPS):
        for z in range(depth):
            for f in range(fields):
                pass_on(step, f, z)
        O, L, R = sides[step + 1]
        for z in range(depth):
            for f in range(fields):
                for copies in gather_copies(step, f, z)[1]:
                    copies[0].wait_recv()
                start = base - first_row - EDGE
                O[f, z] = shifted(windows[step][f, z, first_row:], start - shifts[...], count, start - SMIN)
            start_side(step + 1, O, L, R, z)
        for z in range(depth):
            await_side(step + 1, O, L, R, z)
            state = [wide(O[f, z], edges(O[f, z], L[f, z], R[f, z])) for f in range(fields)]
            if step == STEPS - 1:
                new = viscous(z, state, False)
                for f in range(fields):
                    out[f, z] = new[f][EDGE : EDGE + width]
            else:
                new = viscous(z, state, True)
                A_rows = slice(TILE - EDGE, TILE - EDGE + count)
                for f in range(fields):
                    A[f, z, A_rows, :] = new[f][:, :lanes]
                hydro(
                    step + 1,
                    z,
                    lambda f: A[f, z],
                    lambda f, own: edges(own, *[new[f][EDGE : EDGE + width, lanes:]] * 2),
                )

    for z in range(depth):
        for copy in ring_copies(z):
            copy.wait_send()
        for phase in range(STEPS + 1):
            end_side(phase, *sides[phase], z)
        for step in range(STEPS):
            for f in range(fields):
                onward, inside = gather_copies(step, f, z)
                onward.wait_send()
                for copies in inside:
                    copies[0].wait_send()


def body(mesh, state, shifts):
    n_az, n_rad = mesh.shape["az"], mesh.shape["rad"]
    fields, depth, width, lanes = state.shape
    behind = SMAX + EDGE
    group = behind // width + 1
    window = (group + 1) * width
    count = width + 2 * EDGE
    vmem = lambda rows: pltpu.VMEM((fields, depth, rows, lanes), jnp.float32)
    dma = pltpu.SemaphoreType.DMA
    return pl.pallas_call(
        functools.partial(kernel, n_az, n_rad),
        out_shape=pltpu.VMEM(state.shape, state.dtype),
        in_specs=[pl.BlockSpec(memory_space=pl.ANY), pl.BlockSpec(memory_space=pltpu.VMEM)],
        out_specs=pl.BlockSpec(memory_space=pltpu.VMEM),
        scratch_shapes=[
            vmem(width),
            dma(()),
            vmem(width + 2 * TILE),
            vmem(window),
            vmem(window),
            vmem(count),
            vmem(count),
            vmem(width),
            vmem(width),
            vmem(count),
            vmem(count),
            vmem(count),
            vmem(count),
            dma((2, depth)),
            dma((2, depth)),
            dma((STEPS, group, fields, depth)),
            dma((STEPS, group, fields, depth)),
            dma((STEPS + 1, 2, depth)),
            dma((STEPS + 1, 2, depth)),
        ],
        compiler_params=pltpu.CompilerParams(collective_id=0, has_side_effects=True),
    )(state, shifts.reshape(1, -1))


def solution(mesh):
    in_specs = (P(None, None, "az", "rad"), P("rad"))
    out_specs = P(None, None, "az", "rad")
    return jax.shard_map(
        functools.partial(body, mesh), mesh=mesh, in_specs=in_specs, out_specs=out_specs, check_vma=False
    )
```

```python
import functools

import jax
import jax.numpy as jnp
from jax import lax
from jax.experimental import pallas as pl
from jax.experimental.pallas import tpu as pltpu
from jax.sharding import PartitionSpec as P

STEPS = 2
SMIN = 4
SMAX = 96
EDGE = 4
TILE = 8

GAMMA_GAS = 1.4
COURANT_RADIAL = 0.15
COURANT_AZIMUTH = 0.15
VISCOSITY_COEF = 1.0


def up(x, axis):
    return pltpu.roll(x, x.shape[axis] - 1, axis)


def down(x, axis):
    return pltpu.roll(x, 1, axis)


def face_speeds(velocity, axis, courant):
    face = (0.5 * courant) * (velocity + up(velocity, axis))
    return jnp.maximum(face, 0.0), jnp.minimum(face, 0.0)


def advect(field, speeds, axis):
    low = field - down(field, axis)
    high = up(low, axis)
    product = low * high
    positive = product > 0
    half = jnp.where(positive, product / jnp.where(positive, low + high, 1.0), 0.0)
    flux = speeds[0] * (field + half) + speeds[1] * up(field - half, axis)
    return flux - down(flux, axis)


def push(pressure, density, speed, axis, courant):
    compress = jnp.minimum(up(speed, axis) - down(speed, axis), 0.0)
    total = pressure + VISCOSITY_COEF * density * compress * compress
    work = total * speed
    scale = -0.5 * courant
    return scale * (up(total, axis) - down(total, axis)), scale * (up(work, axis) - down(work, axis))


def shifted(window, shift_left, rows, longest):
    bits = longest.bit_length()
    x = window
    for bit in reversed(range(bits)):
        stride = 1 << bit
        left = stride - 1
        if stride >= TILE:
            keep = -(-(rows + left) // TILE) * TILE
            chosen = min(keep, x.shape[0] - stride)
            mask = (jnp.broadcast_to(shift_left, (chosen, shift_left.shape[1])) & stride) != 0
            y = jnp.where(mask, x[stride : stride + chosen], x[:chosen])
            x = y if chosen == keep else jnp.concatenate([y, x[chosen:keep]], axis=0)
        else:
            mask = (jnp.broadcast_to(shift_left, x.shape) & stride) != 0
            x = jnp.where(mask, pltpu.roll(x, x.shape[0] - stride, 0), x)
    return x[:rows]


def kernel(n_az, n_rad, x_in, shifts, out, *scratch):
    (x, load_sem, A, W0, W1, O0, O1, L0, R0, L1, R1, L2, R2, state_send, state_recv, gather_send, gather_recv,
     side_send, side_recv) = scratch
    fields, depth, width, lanes = x.shape
    behind = SMAX + EDGE
    whole = behind // width
    tail = behind % width
    tail_rows = -(-tail // TILE) * TILE
    group = whole + 1
    base = group * width
    first_row = width - tail_rows
    me = lax.axis_index("az")
    place = lax.rem(me, group)
    position = lax.axis_index("rad")

    def az(by):
        return {"az": lax.rem(me + by + n_az, n_az)}

    def member(by):
        return {"az": me - place + lax.rem(place + by + group, group)}

    def rad(by):
        return {"rad": position + by}

    barrier = pltpu.get_barrier_semaphore()
    MESH = pl.DeviceIdType.MESH
    load = pltpu.make_async_copy(x_in, x, load_sem)
    load.start()
    for by in (1, -1, -group):
        pl.semaphore_signal(barrier, inc=1, device_id=az(by), device_id_type=MESH)
    for h in range(1, group):
        pl.semaphore_signal(barrier, inc=1, device_id=member(h), device_id_type=MESH)

    has_left = position > 0
    has_right = position < n_rad - 1

    @pl.when(has_left)
    def _():
        pl.semaphore_signal(barrier, inc=1, device_id=rad(-1), device_id_type=MESH)

    @pl.when(has_right)
    def _():
        pl.semaphore_signal(barrier, inc=1, device_id=rad(1), device_id_type=MESH)

    load.wait()
    A[:, :, TILE : TILE + width, :] = x[...]
    beside_me = (position + n_rad - 1) // n_rad + (2 * n_rad - 2 - position) // n_rad
    pl.semaphore_wait(barrier, group + 2 + beside_me)

    def remote(src, dst, send, recv, where):
        return pltpu.make_async_remote_copy(
            src_ref=src, dst_ref=dst, send_sem=send, recv_sem=recv, device_id=where, device_id_type=MESH
        )

    def ring_copies(z):
        return [
            remote(x.at[:, z, width - TILE : width], A.at[:, z, 0:TILE],
                   state_send.at[0, z], state_recv.at[0, z], az(1)),
            remote(x.at[:, z, 0:TILE], A.at[:, z, TILE + width : 2 * TILE + width],
                   state_send.at[1, z], state_recv.at[1, z], az(-1)),
        ]

    def side_copies(phase, src, left_dst, right_dst, f, z):
        to_right = remote(src.at[f, z], left_dst.at[f, z], side_send.at[phase, 0, f, z],
                          side_recv.at[phase, 0, f, z], rad(1))
        to_left = remote(src.at[f, z], right_dst.at[f, z], side_send.at[phase, 1, f, z],
                         side_recv.at[phase, 1, f, z], rad(-1))
        return to_right, to_left

    def start_side(*args):
        to_right, to_left = side_copies(*args)

        @pl.when(has_right)
        def _():
            to_right.start()

        @pl.when(has_left)
        def _():
            to_left.start()

    def await_side(*args):
        to_right, to_left = side_copies(*args)

        @pl.when(has_left)
        def _():
            to_right.wait_recv()

        @pl.when(has_right)
        def _():
            to_left.wait_recv()

    def end_side(*args):
        to_right, to_left = side_copies(*args)

        @pl.when(has_right)
        def _():
            to_right.wait_send()

        @pl.when(has_left)
        def _():
            to_left.wait_send()

    windows = (W0, W1)
    rotated = (O0, O1)
    sides = ((x, L0, R0), (O0, L1, R1), (O1, L2, R2))

    def gather_copies(step, f, z):
        W = windows[step]
        own, back = W.at[f, z, base : base + width], W.at[f, z, 0:width]
        sems = lambda h: (gather_send.at[step, h, f, z], gather_recv.at[step, h, f, z])
        onward = remote(own, back, *sems(0), az(group))
        inside = []
        for h in range(1, group):
            dst = W.at[f, z, base - h * width : base - (h - 1) * width]
            inside.append([remote(src, dst, *sems(h), member(h)) for src in (own, back)])
        return onward, inside

    def send_own(step, f, z):
        onward, inside = gather_copies(step, f, z)
        onward.start()
        for h in range(1, group):

            @pl.when(place + h < group)
            def _():
                inside[h - 1][0].start()

    def pass_on(step, f, z):
        onward, inside = gather_copies(step, f, z)
        onward.wait_recv()
        for h in range(1, group):

            @pl.when(place + h >= group)
            def _():
                inside[h - 1][1].start()

    def edges(own, left, right):
        rows = own.shape[0]
        lane = lax.broadcasted_iota(jnp.int32, (rows, lanes), 1)
        at = jnp.full((rows, lanes), position, jnp.int32)
        left = jnp.where(at == 0, jnp.broadcast_to(own[:, 0:1], own.shape), left)
        right = jnp.where(at == n_rad - 1, jnp.broadcast_to(own[:, lanes - 1 : lanes], own.shape), right)
        return jnp.where(lane < lanes // 2, right, left)

    def wide(own, beside):
        return jnp.concatenate([own, beside], axis=1)

    def hydro(step, z, strip, beside):
        rows = slice(TILE, TILE + width)
        tall = [strip(f) for f in range(fields)]
        az_speeds = face_speeds(tall[2] / tall[0], 0, COURANT_AZIMUTH)
        broad = [wide(tall[f][rows], beside(f, tall[f][rows])) for f in range(fields)]
        rad_speeds = face_speeds(broad[1] / broad[0], 1, COURANT_RADIAL)
        for f in range(fields):
            along = advect(tall[f], az_speeds, 0)[rows]
            across = advect(broad[f], rad_speeds, 1)[:, :lanes]
            windows[step][f, z, base : base + width, :] = tall[f][rows] - along - across
            send_own(step, f, z)

    def viscous(z, state, extended):
        rho, mr, mp, mz, energy = state
        own = slice(None) if extended else slice(0, lanes)
        inverse = 1.0 / rho
        pressure = (GAMMA_GAS - 1.0) * (energy - 0.5 * (mr * mr + mp * mp + mz * mz) * inverse)
        az_m, az_e = push(pressure[:, own], rho[:, own], (mp * inverse)[:, own], 0, COURANT_AZIMUTH)
        rad_m, rad_e = push(pressure, rho, mr * inverse, 1, COURANT_RADIAL)
        return [
            rho[:, own],
            mr[:, own] + rad_m[:, own],
            mp[:, own] + az_m,
            mz[:, own],
            energy[:, own] + az_e + rad_e[:, own],
        ]

    count = width + 2 * EDGE

    for z in range(depth):
        for copy in ring_copies(z):
            copy.start()
    for z in range(depth):
        for f in range(fields):
            start_side(0, *sides[0], f, z)
    for z in range(depth):
        for copy in ring_copies(z):
            copy.wait_recv()
        for f in range(fields):
            await_side(0, *sides[0], f, z)
        hydro(0, z, lambda f: A[f, z], lambda f, own: edges(own, L0[f, z], R0[f, z]))

    for step in range(STEPS):
        for z in range(depth):
            for f in range(fields):
                pass_on(step, f, z)
        O, L, R = sides[step + 1]
        for z in range(depth):
            for f in range(fields):
                for copies in gather_copies(step, f, z)[1]:
                    copies[0].wait_recv()
                start = base - first_row - EDGE
                O[f, z] = shifted(windows[step][f, z, first_row:], start - shifts[...], count, start - SMIN)
                start_side(step + 1, O, L, R, f, z)
        for z in range(depth):
            for f in range(fields):
                await_side(step + 1, O, L, R, f, z)
            state = [wide(O[f, z], edges(O[f, z], L[f, z], R[f, z])) for f in range(fields)]
            if step == STEPS - 1:
                new = viscous(z, state, False)
                for f in range(fields):
                    out[f, z] = new[f][EDGE : EDGE + width]
            else:
                new = viscous(z, state, True)
                A_rows = slice(TILE - EDGE, TILE - EDGE + count)
                for f in range(fields):
                    A[f, z, A_rows, :] = new[f][:, :lanes]
                hydro(
                    step + 1,
                    z,
                    lambda f: A[f, z],
                    lambda f, own: edges(own, *[new[f][EDGE : EDGE + width, lanes:]] * 2),
                )

    for z in range(depth):
        for copy in ring_copies(z):
            copy.wait_send()
        for phase in range(STEPS + 1):
            for f in range(fields):
                end_side(phase, *sides[phase], f, z)
        for step in range(STEPS):
            for f in range(fields):
                onward, inside = gather_copies(step, f, z)
                onward.wait_send()
                for copies in inside:
                    copies[0].wait_send()


def body(mesh, state, shifts):
    n_az, n_rad = mesh.shape["az"], mesh.shape["rad"]
    fields, depth, width, lanes = state.shape
    behind = SMAX + EDGE
    group = behind // width + 1
    window = (group + 1) * width
    count = width + 2 * EDGE
    vmem = lambda rows: pltpu.VMEM((fields, depth, rows, lanes), jnp.float32)
    dma = pltpu.SemaphoreType.DMA
    return pl.pallas_call(
        functools.partial(kernel, n_az, n_rad),
        out_shape=pltpu.VMEM(state.shape, state.dtype),
        in_specs=[pl.BlockSpec(memory_space=pl.ANY), pl.BlockSpec(memory_space=pltpu.VMEM)],
        out_specs=pl.BlockSpec(memory_space=pltpu.VMEM),
        scratch_shapes=[
            vmem(width),
            dma(()),
            vmem(width + 2 * TILE),
            vmem(window),
            vmem(window),
            vmem(count),
            vmem(count),
            vmem(width),
            vmem(width),
            vmem(count),
            vmem(count),
            vmem(count),
            vmem(count),
            dma((2, depth)),
            dma((2, depth)),
            dma((STEPS, group, fields, depth)),
            dma((STEPS, group, fields, depth)),
            dma((STEPS + 1, 2, fields, depth)),
            dma((STEPS + 1, 2, fields, depth)),
        ],
        compiler_params=pltpu.CompilerParams(collective_id=0, has_side_effects=True),
    )(state, shifts.reshape(1, -1))


def solution(mesh):
    in_specs = (P(None, None, "az", "rad"), P("rad"))
    out_specs = P(None, None, "az", "rad")
    return jax.shard_map(
        functools.partial(body, mesh), mesh=mesh, in_specs=in_specs, out_specs=out_specs, check_vma=False
    )
```
